32 devices in a mesh: gx: 4 (over x, core), gy: 8 (over z, y).
Axes of the slice: x: 2, y: 2, z: 4, core: 2. Of those that a mesh axis runs over, the one named last changes fastest.
Arguments:
- probes: float32 [32, 64, 64, 256], P(None, 'gx', 'gy'), may hold values from -108 to 108, as said below
- diffusion: float32 [64, 64, 256], P('gx', 'gy'), may hold values from 0.03 to 0.16
- velocity: float32 [3, 64, 64, 256], P(None, 'gx', 'gy'), may hold values from -0.2 to 0.2
Outputs:
- basis: float32 [32, 64, 64, 256], P(None, 'gx', 'gy')
- factor: float32 [32, 32], replicated
The draws below stay inside these ranges and needn't reach their ends.
Inputs may be any that keep to these rules, and one draw needn't show every extreme that they name: `probes`: each entry is finite and real-valued.
All inputs are finite; a program needn't handle non-finite values.
Results may differ from the reference program's by a relative error of at most 0.00011.
Values sent between devices are 32-bit elements; how exact they have to be, the bound alone decides.
No kernel may reach another device: no remote copies, remote signals or barrier semaphores. Data moves between devices by JAX's collectives and lax.ppermute only.
A program may use at most 64 MiB of HBM per device.

```python
import math
import jax
import jax.numpy as jnp
from jax import lax

PROBES = 32
STEPS = 2
NZ = 256
NX = 64
NY = 64
CELLS = 1048576


def draw_probes(key, part):
    keys = jax.random.split(key, 3)
    ramp_x = jnp.exp(math.log(3.0) * jnp.arange(NX, dtype=jnp.float32) / max(NX - 1, 1))
    ramp_y = jnp.exp(math.log(3.0) * jnp.arange(NY, dtype=jnp.float32) / max(NY - 1, 1))
    cell_scale = jnp.exp(jax.random.uniform(keys[1], (NX, NY, NZ), jnp.float32, math.log(0.1), 0.0))
    cell_scale = cell_scale * ramp_x[:, None, None] * ramp_y[None, :, None]
    base = jax.random.truncated_normal(keys[0], -4.0, 4.0, (PROBES, NX, NY, NZ), jnp.float32)
    column = jnp.exp(jax.random.uniform(keys[2], (PROBES,), jnp.float32, math.log(0.3), math.log(3.0)))
    return base * column[:, None, None, None] * cell_scale[None]


def block_levels(rng, extent, cuts, low, largest):
    gain, own = 1.0, jax.random.fold_in(rng, 6)
    for axis_at, blocks in cuts:
        heights = jnp.exp(jax.random.uniform(jax.random.fold_in(own, axis_at), (blocks,), jnp.float32, low / len(cuts), largest / len(cuts)))
        gain = gain * jnp.repeat(heights, extent[axis_at] // blocks).reshape([-1 if axis == axis_at else 1 for axis in range(len(extent))])
    return gain


def setup_inputs(seed: int = 0) -> dict:
    splits = jax.random.split(jax.random.key(seed), 4)
    probes = draw_probes(jax.random.fold_in(splits[3], 71), 0)
    diffusion = jnp.clip(jnp.exp(math.log(0.16) - 1.6739764 * jax.random.uniform(splits[1], (NX, NY, NZ), jnp.float32) ** block_levels(splits[1], (NX, NY, NZ), ((0, 4), (1, 8)), -0.2, 0.2)), 0.03, 0.16)
    velocity = jnp.clip(jax.random.uniform(splits[2], (3, NX, NY, NZ), jnp.float32, -0.2, 0.2) * block_levels(splits[2], (3, NX, NY, NZ), ((1, 4), (2, 8)), -0.4, 0.0), -0.2, 0.2)
    return dict(probes=probes, diffusion=diffusion, velocity=velocity)


def advance(field, diffusion, velocity):
    padded = jnp.pad(field, 1)
    result = (1.0 - 6.0 * diffusion) * field
    result = result + (diffusion - 0.5 * velocity[0]) * padded[2:, 1:-1, 1:-1] + (diffusion + 0.5 * velocity[0]) * padded[:-2, 1:-1, 1:-1]
    result = result + (diffusion - 0.5 * velocity[1]) * padded[1:-1, 2:, 1:-1] + (diffusion + 0.5 * velocity[1]) * padded[1:-1, :-2, 1:-1]
    result = result + (diffusion - 0.5 * velocity[2]) * padded[1:-1, 1:-1, 2:] + (diffusion + 0.5 * velocity[2]) * padded[1:-1, 1:-1, :-2]
    return result

def reference(probes, diffusion, velocity):

    def advance_probe(field):
        for sweep_index in range(STEPS):
            field = advance(field, diffusion, velocity)
        return field
    image = lax.map(advance_probe, probes)
    flat = image.reshape(PROBES, -1)
    gram = jnp.dot(flat.astype(jnp.float32), flat.T.astype(jnp.float32), precision=lax.Precision.HIGHEST, preferred_element_type=jnp.float32) * (1.0 / CELLS)
    lower = jnp.linalg.cholesky(gram)
    basis = jax.scipy.linalg.solve_triangular(lower, flat, lower=True)
    return (basis.reshape(image.shape), lower.T)
```

```python
import functools

import jax
import jax.numpy as jnp
from jax import lax
from jax.experimental import pallas as pl
from jax.experimental.pallas import tpu as pltpu
from jax.sharding import PartitionSpec as P

F32 = jnp.float32
VMEM = pl.BlockSpec(memory_space=pltpu.VMEM)
ANY = pl.BlockSpec(memory_space=pl.ANY)
LANES = 128
W0, XP, XM, YP, YM, ZP, ZM = range(7)


def call(body, outs, ins, scratch=(), in_specs=None, out_specs=None, name=None):
    return pl.pallas_call(
        body,
        out_shape=[jax.ShapeDtypeStruct(s, F32) for s in outs],
        in_specs=in_specs or [VMEM] * len(ins),
        out_specs=out_specs or [VMEM] * len(outs),
        scratch_shapes=list(scratch),
        compiler_params=pltpu.CompilerParams(vmem_limit_bytes=24 << 20),
        name=name,
    )(*ins)


def spread_kernel(nx, ny, np_, nz, p_ref, d_ref, v_ref, u_ref, c_ref, up_ref, dn_ref, xlo_ref, xhi_ref):
    half = nx * np_
    parts = nz // LANES
    for x in range(nx):
        for y in range(ny):
            block = jnp.concatenate(
                [p_ref[pl.ds((x * parts + h) * ny + y, np_, stride=nx * parts * ny), :] for h in range(parts)], axis=1
            )
            u_ref[x, y] = block
            if y == 0:
                dn_ref[x * np_ : (x + 1) * np_, :] = block
            if y == ny - 1:
                up_ref[x * np_ : (x + 1) * np_, :] = block
            if x == 0:
                xlo_ref[y] = block
            if x == nx - 1:
                xhi_ref[y] = block
    d = d_ref[...]
    vx, vy, vz = 0.5 * v_ref[0], 0.5 * v_ref[1], 0.5 * v_ref[2]
    z = lax.broadcasted_iota(jnp.int32, (nx, ny, nz), 2)
    c_ref[W0] = 1.0 - 6.0 * d
    c_ref[XP] = d - vx
    c_ref[XM] = d + vx
    c_ref[YP] = d - vy
    c_ref[YM] = d + vy
    c_ref[ZP] = jnp.where(z == nz - 1, 0.0, d - vz)
    c_ref[ZM] = jnp.where(z == 0, 0.0, d + vz)
    for x in range(nx):
        dn_ref[half + x : half + x + 1, :] = c_ref[YM, x, 0:1, :]
        up_ref[half + x : half + x + 1, :] = c_ref[YP, x, ny - 1 : ny, :]


def sweep(nx, ny, nz, get, c_ref, lo, hi, ring, emit):
    def column(x, before, after):
        rows = [get(x, y) for y in range(ny)]
        for y in range(ny):
            here = rows[y]
            k = lambda i: c_ref[i, x, pl.ds(y, 1), :]
            total = k(W0) * here
            total = total + k(XP) * after(y) + k(XM) * before(y)
            if y + 1 < ny:
                total = total + k(YP) * rows[y + 1]
            elif ring is not None:
                total = total + k(YP) * ring(x, y)
            if y > 0:
                total = total + k(YM) * rows[y - 1]
            elif ring is not None:
                total = total + k(YM) * ring(x, y)
            total = total + k(ZP) * pltpu.roll(here, nz - 1, 1) + k(ZM) * pltpu.roll(here, 1, 1)
            emit(x, y, total)

    column(0, lambda y: lo[y], lambda y: get(1, y))

    @pl.loop(1, nx - 1)
    def _(x):
        column(x, lambda y: get(x - 1, y), lambda y: get(x + 1, y))

    column(nx - 1, lambda y: get(nx - 2, y), lambda y: hi[y])


def split(ny, low, inner, high):
    def get(x, y):
        return low[x] if y == 0 else high[x] if y == ny - 1 else inner[x, y - 1]

    def put(x, y, value):
        if y == 0:
            low[x] = value
        elif y == ny - 1:
            high[x] = value
        else:
            inner[x, y - 1] = value

    return get, put


def first_kernel(nx, ny, nz, u_ref, c_ref, lo_ref, hi_ref, v_ref, dn_ref, up_ref):
    _, put = split(ny, dn_ref, v_ref, up_ref)
    sweep(nx, ny, nz, lambda x, y: u_ref[x, y], c_ref, lo_ref, hi_ref, None, put)


def close_kernel(nx, ny, np_, c_ref, below_ref, above_ref, v_ref, dn_ref, up_ref, low_ref, high_ref, xlo_ref, xhi_ref):
    last = ny - 1
    for x in range(nx):
        rows = slice(x * np_, (x + 1) * np_)
        low_ref[x] = dn_ref[x] + c_ref[YM, x, 0:1, :] * below_ref[rows, :]
        high_ref[x] = up_ref[x] + c_ref[YP, x, last : last + 1, :] * above_ref[rows, :]
    get, _ = split(ny, low_ref, v_ref, high_ref)
    for y in range(ny):
        xlo_ref[y] = get(0, y)
        xhi_ref[y] = get(nx - 1, y)


def dot(a, b, dims):
    return lax.dot_general(a, b, (dims, ((), ())), precision=lax.Precision.HIGHEST, preferred_element_type=F32)


def second_kernel(
    nx, ny, np_, nz, u_ref, v_ref, vlow_ref, vhigh_ref, c_ref, below_ref, above_ref, lo_ref, hi_ref,
    w_ref, wlow_ref, whigh_ref, g_ref,
):
    half = nx * np_
    get, _ = split(ny, vlow_ref, v_ref, vhigh_ref)
    _, put = split(ny, wlow_ref, w_ref, whigh_ref)

    def ring(x, y):
        side = below_ref if y == 0 else above_ref
        return side[pl.ds(half + x, 1), :] * u_ref[x, y]

    g_ref[...] = jnp.zeros_like(g_ref)

    def emit(x, y, total):
        put(x, y, total)
        if 0 < y < ny - 1:
            g_ref[...] += dot(total, total, ((1,), (1,)))

    sweep(nx, ny, nz, get, c_ref, lo_ref, hi_ref, ring, emit)


def last_kernel(nx, ny, np_, copies, c_ref, below_ref, above_ref, g_in, wlow_in, whigh_in, wlow_ref, whigh_ref, g_ref):
    last = ny - 1
    gram = g_in[...]
    for x in range(nx):
        low = wlow_in[x] + c_ref[YM, x, 0:1, :] * below_ref[x]
        wlow_ref[x] = low
        gram = gram + dot(low, low, ((1,), (1,)))
        high = whigh_in[x] + c_ref[YP, x, last : last + 1, :] * above_ref[x]
        whigh_ref[x] = high
        gram = gram + dot(high, high, ((1,), (1,)))
    packed = jnp.concatenate([gram[8 * i : 8 * i + 8, :] for i in range(np_ // 8)], axis=1)
    for i in range(copies):
        g_ref[i] = packed


def basis_kernel(nx, ny, np_, scale, g_ref, w_ref, wlow_ref, whigh_ref, out_ref, factor_ref, inv_ref, stage, sems):
    get, _ = split(ny, wlow_ref, w_ref, whigh_ref)
    n = np_
    total = jnp.sum(g_ref[...], axis=0) * scale
    gram = jnp.concatenate([total[:, n * i : n * i + n] for i in range(n // 8)], axis=0)
    lane = lax.broadcasted_iota(jnp.int32, (1, n), 1)
    sub = lax.broadcasted_iota(jnp.int32, (n, 1), 0)
    right = jnp.where(lax.broadcasted_iota(jnp.int32, (n, n), 0) == lax.broadcasted_iota(jnp.int32, (n, n), 1), 1.0, 0.0)
    left = gram
    for k in range(n):
        r = lax.rsqrt(left[k : k + 1, k : k + 1])
        frow = left[k : k + 1, :] * r
        irow = right[k : k + 1, :] * r
        factor_ref[k : k + 1, :] = jnp.where(lane >= k, frow, 0.0)
        inv_ref[k : k + 1, :] = irow
        if k + 1 < n:
            col = jnp.where(sub > k, left[:, k : k + 1] * r, 0.0)
            left = left - col * frow
            right = right - col * irow
    inv = inv_ref[...]
    parts = wlow_ref.shape[2] // LANES
    group = parts * ny

    def copy(x):
        return pltpu.make_async_copy(stage.at[x % 2].reshape(n, group, LANES), out_ref.at[:, x], sems.at[x % 2])

    for x in range(nx):
        if x >= 2:
            copy(x - 2).wait()
        for y in range(ny):
            block = dot(inv, get(x, y), ((1,), (0,)))
            for h in range(parts):
                stage.at[x % 2][pl.ds(h * ny + y, n, stride=group), :] = block[:, h * LANES : (h + 1) * LANES]
        copy(x).start()
    copy(nx - 2).wait()
    copy(nx - 1).wait()


def on_device(probes, diffusion, velocity):
    np_, nx, ny, nz = probes.shape
    mx, my = lax.axis_size("gx"), lax.axis_size("gy")
    cells = mx * my * nx * ny * nz
    grid = (nx, ny, np_, nz)
    inner = (nx, ny - 2, np_, nz)
    plane = (nx, np_, nz)
    face = (ny, np_, nz)
    tall = (nx * np_ + nx, nz)
    up_x = [(i, i + 1) for i in range(mx - 1)]
    dn_x = [(i + 1, i) for i in range(mx - 1)]
    up_y = [(i, i + 1) for i in range(my - 1)]
    dn_y = [(i + 1, i) for i in range(my - 1)]

    parts = nz // LANES
    rows = probes.reshape(np_, nx, ny, parts, LANES).transpose(0, 1, 3, 2, 4).reshape(-1, LANES)
    u, coef, up, dn, xlo, xhi = call(
        functools.partial(spread_kernel, nx, ny, np_, nz),
        [grid, (7, nx, ny, nz), tall, tall, face, face],
        [rows, diffusion, velocity],
        name="spread",
    )
    below = lax.ppermute(up, "gy", up_y)
    above = lax.ppermute(dn, "gy", dn_y)
    before = lax.ppermute(xhi, "gx", up_x)
    after = lax.ppermute(xlo, "gx", dn_x)
    v, dn2, up2 = call(
        functools.partial(first_kernel, nx, ny, nz),
        [inner, plane, plane],
        [u, coef, before, after],
        name="first",
    )
    below2 = lax.ppermute(up2, "gy", up_y)
    above2 = lax.ppermute(dn2, "gy", dn_y)
    vlow, vhigh, xlo2, xhi2 = call(
        functools.partial(close_kernel, nx, ny, np_),
        [plane, plane, face, face],
        [coef, below, above, v, dn2, up2],
        name="close",
    )
    before2 = lax.ppermute(xhi2, "gx", up_x)
    after2 = lax.ppermute(xlo2, "gx", dn_x)
    w, wlow, whigh, gram = call(
        functools.partial(second_kernel, nx, ny, np_, nz),
        [inner, plane, plane, (np_, np_)],
        [u, v, vlow, vhigh, coef, below, above, before2, after2],
        name="second",
    )
    wlow, whigh, grams = call(
        functools.partial(last_kernel, nx, ny, np_, mx * my),
        [plane, plane, (mx * my, 8, np_ * np_ // 8)],
        [coef, below2, above2, gram, wlow, whigh],
        name="last",
    )
    grams = lax.all_to_all(grams, ("gx", "gy"), 0, 0, tiled=True)
    basis, factor = call(
        functools.partial(basis_kernel, nx, ny, np_, 1.0 / cells),
        [(np_, nx, parts * ny, LANES), (np_, np_)],
        [grams, w, wlow, whigh],
        scratch=[
            pltpu.VMEM((np_, np_), F32),
            pltpu.VMEM((2, np_ * parts * ny, LANES), F32),
            pltpu.SemaphoreType.DMA((2,)),
        ],
        out_specs=[ANY, VMEM],
        name="basis",
    )
    basis = basis.reshape(np_, nx, parts, ny, LANES).transpose(0, 1, 3, 2, 4).reshape(np_, nx, ny, nz)
    return basis, factor


def solution(mesh):
    return jax.shard_map(
        on_device,
        mesh=mesh,
        in_specs=(P(None, "gx", "gy", None), P("gx", "gy", None), P(None, "gx", "gy", None)),
        out_specs=(P(None, "gx", "gy", None), P()),
        check_vma=False,
    )
```

```python
import functools

import jax
import jax.numpy as jnp
from jax import lax
from jax.experimental import pallas as pl
from jax.experimental.pallas import tpu as pltpu
from jax.sharding import PartitionSpec as P

F32 = jnp.float32
BF16 = jnp.bfloat16
VMEM = pl.BlockSpec(memory_space=pltpu.VMEM)
ANY = pl.BlockSpec(memory_space=pl.ANY)
LANES = 128
BLOCK = 8
W0, XP, XM, YP, YM, ZP, ZM = range(7)


def call(body, outs, ins, scratch=(), in_specs=None, out_specs=None, name=None, vmem=24):
    return pl.pallas_call(
        body,
        out_shape=[jax.ShapeDtypeStruct(s, F32) for s in outs],
        in_specs=in_specs or [VMEM] * len(ins),
        out_specs=out_specs or [VMEM] * len(outs),
        scratch_shapes=list(scratch),
        compiler_params=pltpu.CompilerParams(vmem_limit_bytes=vmem << 20),
        name=name,
    )(*ins)


def edge_kernel(nx, ny, np_, parts, p_ref, d_ref, v_ref, up_ref, dn_ref, xlo_ref, xhi_ref, terms, sem):
    last = ny - 1
    half = nx * np_
    copies = []
    for x in range(nx):
        rows = pl.ds(x * np_, np_)
        for h in range(parts):
            lanes = pl.ds(h * LANES, LANES)
            copies.append((p_ref.at[:, x, h, last, :], up_ref.at[rows, lanes]))
            copies.append((p_ref.at[:, x, h, 0, :], dn_ref.at[rows, lanes]))
    for h in range(parts):
        for i, y in enumerate((0, last)):
            copies.append((d_ref.at[:, h, y, :], terms.at[i, :, pl.ds(h * LANES, LANES)]))
            copies.append((v_ref.at[1, :, h, y, :], terms.at[2 + i, :, pl.ds(h * LANES, LANES)]))
    layers = np_ * 2 * parts * ny
    some = parts * ny
    for ref, first, outer in ((xlo_ref, 0, 0), (xhi_ref, nx - 2, nx - 1)):
        face = ref.at[pl.ds(0, layers)].reshape(np_, 2, parts, ny, LANES)
        copies.append((p_ref.at[:, pl.ds(first, 2)], face))
        copies.append((d_ref.at[outer], ref.at[pl.ds(layers, some)].reshape(parts, ny, LANES)))
        copies.append((v_ref.at[:, outer], ref.at[pl.ds(layers + some, 3 * some)].reshape(3, parts, ny, LANES)))
    copies = [pltpu.make_async_copy(src, dst, sem) for src, dst in copies]
    for copy in copies:
        copy.start()
    for copy in copies:
        copy.wait()
    dn_ref[half : half + nx, :] = terms[0] + 0.5 * terms[2]
    up_ref[half : half + nx, :] = terms[1] - 0.5 * terms[3]


def coefficients(d, vx, vy, vz):
    z = lax.broadcasted_iota(jnp.int32, d.shape, d.ndim - 1)
    return (
        1.0 - 6.0 * d,
        d - 0.5 * vx,
        d + 0.5 * vx,
        d - 0.5 * vy,
        d + 0.5 * vy,
        jnp.where(z == d.shape[-1] - 1, 0.0, d - 0.5 * vz),
        jnp.where(z == 0, 0.0, d + 0.5 * vz),
    )


def spread_kernel(nx, ny, np_, nz, p_ref, d_ref, v_ref, u_ref, c_ref):
    parts = nz // LANES
    for x in range(nx):
        for y in range(ny):
            for h in range(parts):
                block = p_ref[pl.ds((x * parts + h) * ny + y, np_, stride=nx * parts * ny), :]
                u_ref[x, y, :, h * LANES : (h + 1) * LANES] = block
    for i, c in enumerate(coefficients(d_ref[...], v_ref[0], v_ref[1], v_ref[2])):
        c_ref[i] = c


def column(ny, nz, ys, row, before, after, coef, ring, emit):
    rows = {y: row(y) for y in sorted({n for y in ys for n in (y - 1, y, y + 1) if 0 <= n < ny})}
    for y in ys:
        here = rows[y]
        k = lambda i: coef(i, y)
        total = k(W0) * here
        total = total + k(XP) * after(y) + k(XM) * before(y)
        if y + 1 < ny:
            total = total + k(YP) * rows[y + 1]
        elif ring is not None:
            total = total + k(YP) * ring(y)
        if y > 0:
            total = total + k(YM) * rows[y - 1]
        elif ring is not None:
            total = total + k(YM) * ring(y)
        total = total + k(ZP) * pltpu.roll(here, nz - 1, 1) + k(ZM) * pltpu.roll(here, 1, 1)
        emit(y, total)


def sweep(nx, ny, nz, ys, get, c_ref, lo, hi, ring, emit):
    def at(x, before, after):
        outside = None if ring is None else lambda y: ring(x, y)
        coef = lambda i, y: c_ref[i, x, pl.ds(y, 1), :]
        column(ny, nz, ys, lambda y: get(x, y), before, after, coef, outside, lambda y, total: emit(x, y, total))

    at(0, lo, lambda y: get(1, y))

    @pl.loop(1, nx - 1)
    def _(x):
        at(x, lambda y: get(x - 1, y), lambda y: get(x + 1, y))

    at(nx - 1, lambda y: get(nx - 2, y), hi)


def split(ny, low, inner, high):
    def get(x, y):
        return low[x] if y == 0 else high[x] if y == ny - 1 else inner[x, y - 1]

    def put(x, y, value):
        if y == 0:
            low[x] = value
        elif y == ny - 1:
            high[x] = value
        else:
            inner[x, y - 1] = value

    return get, put


def first_kernel(nx, ny, np_, nz, u_ref, c_ref, lo_ref, hi_ref, v_ref, dn_ref, up_ref, vlo_ref, vhi_ref, k_ref):
    parts = nz // LANES
    layers = np_ * 2 * parts * ny

    def layer(ref, i):
        def get(y):
            each = [ref[pl.ds((i * parts + h) * ny + y, np_, stride=2 * parts * ny), :] for h in range(parts)]
            return jnp.concatenate(each, axis=1)

        return get

    for side, ref in enumerate((lo_ref, hi_ref)):
        tile = lambda i: jnp.concatenate(
            [ref[layers + (i * parts + h) * ny : layers + (i * parts + h + 1) * ny, :] for h in range(parts)], axis=1
        )
        for i, c in enumerate(coefficients(tile(0), tile(1), tile(2), tile(3))):
            k_ref[side, i] = c

    def outer(side, row, before, after, out_ref):
        def emit(y, total):
            out_ref[y] = total

        column(ny, nz, range(ny), row, before, after, lambda i, y: k_ref[side, i, pl.ds(y, 1), :], None, emit)

    get = lambda x, y: u_ref[x, y]
    outer(0, layer(lo_ref, 1), layer(lo_ref, 0), lambda y: get(0, y), vlo_ref)
    outer(1, layer(hi_ref, 0), lambda y: get(nx - 1, y), layer(hi_ref, 1), vhi_ref)
    _, put = split(ny, dn_ref, v_ref, up_ref)
    sweep(nx, ny, nz, range(ny), get, c_ref, layer(lo_ref, 1), layer(hi_ref, 0), None, put)


def close_kernel(nx, ny, np_, c_ref, below_ref, above_ref, dn_ref, up_ref, low_ref, high_ref, xlo_ref, xhi_ref):
    last = ny - 1
    for x in range(nx):
        rows = slice(x * np_, (x + 1) * np_)
        low = c_ref[YM, x, 0:1, :] * below_ref[rows, :]
        high = c_ref[YP, x, last : last + 1, :] * above_ref[rows, :]
        low_ref[x] = dn_ref[x] + low
        high_ref[x] = up_ref[x] + high
        if x == 0:
            xlo_ref[0], xlo_ref[1] = low, high
        if x == nx - 1:
            xhi_ref[0], xhi_ref[1] = low, high


def pieces(a):
    high = a.astype(BF16)
    rest = a - high.astype(F32)
    mid = rest.astype(BF16)
    return high, mid, (rest - mid.astype(F32)).astype(BF16)


def square(a):
    stack = jnp.concatenate(pieces(a), axis=0)
    return lax.dot_general(stack, stack, (((1,), (1,)), ((), ())), preferred_element_type=F32)


def fold(n, a):
    block = lambda i, j: a[i * n : i * n + n, j * n : j * n + n]
    return block(0, 0) + ((block(0, 1) + block(1, 0)) + (block(1, 1) + (block(0, 2) + block(2, 0))))


def face(ref):
    return lambda y: ref[y]


def middle_kernel(nx, ny, nz, v_ref, c_ref, lo_ref, hi_ref, dn_ref, up_ref, w_ref, g_ref, dn_out, up_out):
    g_ref[...] = jnp.zeros_like(g_ref)

    def emit(x, y, total):
        w_ref[x, y - 2] = total
        g_ref[...] += square(total)

    sweep(nx, ny, nz, range(2, ny - 2), lambda x, y: v_ref[x, y - 1], c_ref, face(lo_ref), face(hi_ref), None, emit)
    dn_out[...] = dn_ref[...]
    up_out[...] = up_ref[...]


def border_kernel(
    nx, ny, np_, nz, u_ref, v_ref, vlow_ref, vhigh_ref, c_ref, below_ref, above_ref, lo_ref, hi_ref,
    w_ref, wlow_ref, whigh_ref, g_ref,
):
    half = nx * np_
    get, _ = split(ny, vlow_ref, v_ref, vhigh_ref)

    def ring(x, y):
        side = below_ref if y == 0 else above_ref
        return side[pl.ds(half + x, 1), :] * u_ref[x, y]

    g_ref[...] = jnp.zeros_like(g_ref)

    def emit(x, y, total):
        if y == 0:
            wlow_ref[x] = total
        elif y == ny - 1:
            whigh_ref[x] = total
        else:
            w_ref[x, 0 if y == 1 else 1] = total
            g_ref[...] += square(total)

    sweep(nx, ny, nz, (0, 1, ny - 2, ny - 1), get, c_ref, face(lo_ref), face(hi_ref), ring, emit)


def last_kernel(
    nx, ny, np_, copies, c_ref, below_ref, above_ref, lo_ref, hi_ref, ga_ref, gb_ref, wlow_in, whigh_in,
    wlow_ref, whigh_ref, g_ref,
):
    last = ny - 1
    gram = ga_ref[...] + gb_ref[...]
    for x in range(nx):
        low = wlow_in[x] + c_ref[YM, x, 0:1, :] * below_ref[x]
        high = whigh_in[x] + c_ref[YP, x, last : last + 1, :] * above_ref[x]
        if x == 0:
            low = low + c_ref[XM, x, 0:1, :] * lo_ref[0]
            high = high + c_ref[XM, x, last : last + 1, :] * lo_ref[1]
        if x == nx - 1:
            low = low + c_ref[XP, x, 0:1, :] * hi_ref[0]
            high = high + c_ref[XP, x, last : last + 1, :] * hi_ref[1]
        wlow_ref[x] = low
        whigh_ref[x] = high
        gram = gram + (square(low) + square(high))
    gram = fold(np_, gram)
    packed = jnp.concatenate([gram[8 * i : 8 * i + 8, :] for i in range(np_ // 8)], axis=1)
    for i in range(copies):
        g_ref[i] = packed


def factor_and_inverse(n, gram, factor_ref, inv_ref):
    eye = lax.broadcasted_iota(jnp.int32, (n, n), 0) == lax.broadcasted_iota(jnp.int32, (n, n), 1)
    a = jnp.concatenate([gram, jnp.where(eye, 1.0, 0.0)], axis=1)
    sub = lax.broadcasted_iota(jnp.int32, (n, 2 * n), 0)
    lane = lax.broadcasted_iota(jnp.int32, (1, n), 1)
    for k0 in range(0, n, BLOCK):
        cols = [jnp.broadcast_to(a[k0:, k : k + 1], (n - k0, 2 * n)) for k in range(k0, k0 + BLOCK)]
        low, rows = a[k0:], sub[k0:]
        for j in range(BLOCK):
            k = k0 + j
            r = lax.rsqrt(cols[j][j : j + 1, :])
            row = low[j : j + 1, :] * r
            factor_ref[k : k + 1, :] = jnp.where(lane >= k, row[:, :n], 0.0)
            inv_ref[k : k + 1, :] = row[:, n:]
            col = jnp.where(rows > k, cols[j] * r, 0.0)
            for m in range(j + 1, BLOCK):
                cols[m] = cols[m] - col * (cols[m][j : j + 1, :] * r)
            low = low - col * row
        a = low if k0 == 0 else jnp.concatenate([a[:k0], low], axis=0)


def basis_kernel(
    nx, ny, np_, scale, g_ref, w_ref, wside_ref, wlow_ref, whigh_ref, out_ref, factor_ref, inv_ref, stage, sems
):
    def get(x, y):
        if y in (0, ny - 1):
            return wlow_ref[x] if y == 0 else whigh_ref[x]
        if y in (1, ny - 2):
            return wside_ref[x, 0 if y == 1 else 1]
        return w_ref[x, y - 2]

    n = np_
    total = jnp.sum(g_ref[...], axis=0) * scale
    gram = jnp.concatenate([total[:, n * i : n * i + n] for i in range(n // 8)], axis=0)
    factor_and_inverse(n, gram, factor_ref, inv_ref)
    high, mid, low = pieces(inv_ref[...])
    none = jnp.zeros_like(high)
    left = jnp.concatenate(
        [jnp.concatenate(row, axis=1) for row in ((high, high, high), (mid, mid, none), (low, none, none))], axis=0
    )
    parts = wlow_ref.shape[2] // LANES
    group = parts * ny
    copies = []
    for x in range(nx):
        for y in range(ny):
            right = jnp.concatenate(pieces(get(x, y)), axis=0)
            terms = lax.dot_general(left, right, (((1,), (0,)), ((), ())), preferred_element_type=F32)
            block = terms[:n] + (terms[n : 2 * n] + terms[2 * n :])
            for h in range(parts):
                stage.at[x][pl.ds(h * ny + y, n, stride=group), :] = block[:, h * LANES : (h + 1) * LANES]
        copy = pltpu.make_async_copy(stage.at[x].reshape(n, group, LANES), out_ref.at[:, x], sems.at[x])
        copy.start()
        copies.append(copy)
    for copy in copies:
        copy.wait()


def on_device(probes, diffusion, velocity):
    np_, nx, ny, nz = probes.shape
    mx, my = lax.axis_size("gx"), lax.axis_size("gy")
    cells = mx * my * nx * ny * nz
    grid = (nx, ny, np_, nz)
    corner = (2, np_, nz)
    square_sum = (3 * np_, 3 * np_)
    plane = (nx, np_, nz)
    face_shape = (ny, np_, nz)
    tall = (nx * np_ + nx, nz)
    up_x = [(i, i + 1) for i in range(mx - 1)]
    dn_x = [(i + 1, i) for i in range(mx - 1)]
    up_y = [(i, i + 1) for i in range(my - 1)]
    dn_y = [(i + 1, i) for i in range(my - 1)]

    parts = nz // LANES
    tiled = lambda a: jnp.swapaxes(a.reshape(a.shape[:-1] + (parts, LANES)), -2, -3)
    tiles = tiled(probes)
    wide = ((2 * np_ + 4) * parts * ny, LANES)
    up, dn, xlo, xhi = call(
        functools.partial(edge_kernel, nx, ny, np_, parts),
        [tall, tall, wide, wide],
        [tiles, tiled(diffusion), tiled(velocity)],
        scratch=[pltpu.VMEM((4, nx, nz), F32), pltpu.SemaphoreType.DMA],
        in_specs=[pl.BlockSpec(memory_space=pltpu.HBM)] * 3,
        name="edge",
        vmem=61,
    )
    below = lax.ppermute(up, "gy", up_y)
    above = lax.ppermute(dn, "gy", dn_y)
    before = lax.ppermute(xhi, "gx", up_x)
    after = lax.ppermute(xlo, "gx", dn_x)
    u, coef = call(
        functools.partial(spread_kernel, nx, ny, np_, nz),
        [grid, (7, nx, ny, nz)],
        [tiles.reshape(-1, LANES), diffusion, velocity],
        name="spread",
    )
    v, dn2, up2, vlo, vhi = call(
        functools.partial(first_kernel, nx, ny, np_, nz),
        [(nx, ny - 2, np_, nz), plane, plane, face_shape, face_shape],
        [u, coef, before, after],
        scratch=[pltpu.VMEM((2, 7, ny, nz), F32)],
        name="first",
    )
    w, gram, dn2, up2 = call(
        functools.partial(middle_kernel, nx, ny, nz),
        [(nx, ny - 4, np_, nz), square_sum, plane, plane],
        [v, coef, vlo, vhi, dn2, up2],
        name="middle",
    )
    below2 = lax.ppermute(up2, "gy", up_y)
    above2 = lax.ppermute(dn2, "gy", dn_y)
    vlow, vhigh, xlo3, xhi3 = call(
        functools.partial(close_kernel, nx, ny, np_),
        [plane, plane, corner, corner],
        [coef, below, above, dn2, up2],
        name="close",
    )
    before3 = lax.ppermute(xhi3, "gx", up_x)
    after3 = lax.ppermute(xlo3, "gx", dn_x)
    wside, wlow, whigh, gram2 = call(
        functools.partial(border_kernel, nx, ny, np_, nz),
        [(nx, 2, np_, nz), plane, plane, square_sum],
        [u, v, vlow, vhigh, coef, below, above, vlo, vhi],
        name="border",
    )
    wlow, whigh, grams = call(
        functools.partial(last_kernel, nx, ny, np_, mx * my),
        [plane, plane, (mx * my, 8, np_ * np_ // 8)],
        [coef, below2, above2, before3, after3, gram, gram2, wlow, whigh],
        name="last",
    )
    grams = lax.all_to_all(grams, ("gx", "gy"), 0, 0, tiled=True)
    basis, factor = call(
        functools.partial(basis_kernel, nx, ny, np_, 1.0 / cells),
        [(np_, nx, parts * ny, LANES), (np_, np_)],
        [grams, w, wside, wlow, whigh],
        scratch=[
            pltpu.VMEM((np_, np_), F32),
            pltpu.VMEM((nx, np_ * parts * ny, LANES), F32),
            pltpu.SemaphoreType.DMA((nx,)),
        ],
        out_specs=[ANY, VMEM],
        name="basis",
    )
    basis = basis.reshape(np_, nx, parts, ny, LANES).transpose(0, 1, 3, 2, 4).reshape(np_, nx, ny, nz)
    return basis, factor


def solution(mesh):
    return jax.shard_map(
        on_device,
        mesh=mesh,
        in_specs=(P(None, "gx", "gy", None), P("gx", "gy", None), P(None, "gx", "gy", None)),
        out_specs=(P(None, "gx", "gy", None), P()),
        check_vma=False,
    )
```

```python
import functools

import jax
import jax.numpy as jnp
from jax import lax
from jax.experimental import pallas as pl
from jax.experimental.pallas import tpu as pltpu
from jax.sharding import PartitionSpec as P

F32 = jnp.float32
BF16 = jnp.bfloat16
VMEM = pl.BlockSpec(memory_space=pltpu.VMEM)
ANY = pl.BlockSpec(memory_space=pl.ANY)
LANES = 128
BLOCK = 8
W0, XP, XM, YP, YM, ZP, ZM = range(7)


def call(body, outs, ins, scratch=(), in_specs=None, out_specs=None, name=None, vmem=24, aliases=None):
    return pl.pallas_call(
        body,
        out_shape=[jax.ShapeDtypeStruct(s, F32) for s in outs],
        in_specs=in_specs or [VMEM] * len(ins),
        out_specs=out_specs or [VMEM] * len(outs),
        scratch_shapes=list(scratch),
        input_output_aliases=aliases or {},
        compiler_params=pltpu.CompilerParams(vmem_limit_bytes=vmem << 20),
        name=name,
    )(*ins)


def move(pairs, sem):
    copies = [pltpu.make_async_copy(src, dst, sem) for src, dst in pairs]
    for copy in copies:
        copy.start()
    for copy in copies:
        copy.wait()


def edge_kernel(nx, ny, np_, parts, p_ref, d_ref, v_ref, up_ref, dn_ref, terms, sem):
    last = ny - 1
    half = nx * np_
    copies = []
    for x in range(nx):
        rows = pl.ds(x * np_, np_)
        for h in range(parts):
            lanes = pl.ds(h * LANES, LANES)
            copies.append((p_ref.at[:, x, h, last, :], up_ref.at[rows, lanes]))
            copies.append((p_ref.at[:, x, h, 0, :], dn_ref.at[rows, lanes]))
    for h in range(parts):
        for i, y in enumerate((0, last)):
            copies.append((d_ref.at[:, h, y, :], terms.at[i, :, pl.ds(h * LANES, LANES)]))
            copies.append((v_ref.at[1, :, h, y, :], terms.at[2 + i, :, pl.ds(h * LANES, LANES)]))
    move(copies, sem)
    dn_ref[half : half + nx, :] = terms[0] + 0.5 * terms[2]
    up_ref[half : half + nx, :] = terms[1] - 0.5 * terms[3]


def side_kernel(nx, ny, np_, parts, p_ref, d_ref, v_ref, lo_ref, hi_ref, sem):
    layers = np_ * 2 * parts * ny
    some = parts * ny
    copies = []
    for ref, first, outer in ((lo_ref, 0, 0), (hi_ref, nx - 2, nx - 1)):
        copies.append((p_ref.at[:, pl.ds(first, 2)], ref.at[pl.ds(0, layers)].reshape(np_, 2, parts, ny, LANES)))
        copies.append((d_ref.at[outer], ref.at[pl.ds(layers, some)].reshape(parts, ny, LANES)))
        copies.append((v_ref.at[:, outer], ref.at[pl.ds(layers + some, 3 * some)].reshape(3, parts, ny, LANES)))
    move(copies, sem)


def coefficients(d, vx, vy, vz):
    z = lax.broadcasted_iota(jnp.int32, d.shape, d.ndim - 1)
    return (
        1.0 - 6.0 * d,
        d - 0.5 * vx,
        d + 0.5 * vx,
        d - 0.5 * vy,
        d + 0.5 * vy,
        jnp.where(z == d.shape[-1] - 1, 0.0, d - 0.5 * vz),
        jnp.where(z == 0, 0.0, d + 0.5 * vz),
    )


def spread(nx, ny, np_, parts, p_ref, u_ref):
    for x in range(nx):
        for y in range(ny):
            for h in range(parts):
                block = p_ref[pl.ds((x * parts + h) * ny + y, np_, stride=nx * parts * ny), :]
                u_ref[x, y, :, h * LANES : (h + 1) * LANES] = block


def coefficient_kernel(d_ref, v_ref, c_ref):
    for i, c in enumerate(coefficients(d_ref[...], v_ref[0], v_ref[1], v_ref[2])):
        c_ref[i] = c


def column(ny, nz, ys, row, before, after, coef, ring, emit):
    rows = {y: row(y) for y in sorted({n for y in ys for n in (y - 1, y, y + 1) if 0 <= n < ny})}
    for y in ys:
        here = rows[y]
        k = lambda i: coef(i, y)
        total = k(W0) * here
        total = total + k(XP) * after(y) + k(XM) * before(y)
        if y + 1 < ny:
            total = total + k(YP) * rows[y + 1]
        elif ring is not None:
            total = total + k(YP) * ring(y)
        if y > 0:
            total = total + k(YM) * rows[y - 1]
        elif ring is not None:
            total = total + k(YM) * ring(y)
        total = total + k(ZP) * pltpu.roll(here, nz - 1, 1) + k(ZM) * pltpu.roll(here, 1, 1)
        emit(y, total)


def sweep(nx, ny, nz, ys, get, c_ref, lo, hi, ring, emit, loop=None, ends=None):
    def at(x, before, after):
        outside = None if ring is None else lambda y: ring(x, y)
        coef = lambda i, y: c_ref[i, x, pl.ds(y, 1), :]
        column(ny, nz, ys, lambda y: get(x, y), before, after, coef, outside, lambda y, total: emit(x, y, total))

    for x in ends:
        at(x, lo if x == 0 else lambda y: get(x - 1, y), hi if x == nx - 1 else lambda y: get(x + 1, y))
    if loop is not None:

        @pl.loop(*loop)
        def _(x):
            at(x, lambda y: get(x - 1, y), lambda y: get(x + 1, y))


def split(ny, low, inner, high):
    def get(x, y):
        return low[x] if y == 0 else high[x] if y == ny - 1 else inner[x, y - 1]

    def put(x, y, value):
        if y == 0:
            low[x] = value
        elif y == ny - 1:
            high[x] = value
        else:
            inner[x, y - 1] = value

    return get, put


def face(ref):
    return lambda y: ref[y]


def layer(ref, i, parts, ny, np_):
    def get(y):
        each = [ref[pl.ds((i * parts + h) * ny + y, np_, stride=2 * parts * ny), :] for h in range(parts)]
        return jnp.concatenate(each, axis=1)

    return get


def face(ref):
    return lambda y: ref[y]


def first_kernel(nx, ny, np_, nz, p_ref, d_ref, v_ref, u_ref, c_ref, out_ref, dn_ref, up_ref, w_ref, g_ref):
    spread(nx, ny, np_, nz // LANES, p_ref, u_ref)
    coefficient_kernel(d_ref, v_ref, c_ref)
    get, put = split(ny, dn_ref, out_ref, up_ref)
    sweep(nx, ny, nz, range(ny), lambda x, y: u_ref[x, y], c_ref, None, None, None, put, (1, nx - 1), ())
    g_ref[...] = jnp.zeros_like(g_ref)

    def emit(x, y, total):
        w_ref[x - 2, y - 2] = total
        g_ref[...] += square(total)

    sweep(nx, ny, nz, range(2, ny - 2), get, c_ref, None, None, None, emit, (2, nx - 2), ())


def outer_kernel(
    nx, ny, np_, nz, u_ref, c_ref, lo_ref, hi_ref, v_in, dn_in, up_in, v_ref, dn_ref, up_ref, vlo_ref, vhi_ref, k_ref
):
    parts = nz // LANES
    layers = np_ * 2 * parts * ny
    for side, ref in enumerate((lo_ref, hi_ref)):
        tile = lambda i: jnp.concatenate(
            [ref[layers + (i * parts + h) * ny : layers + (i * parts + h + 1) * ny, :] for h in range(parts)], axis=1
        )
        for i, c in enumerate(coefficients(tile(0), tile(1), tile(2), tile(3))):
            k_ref[side, i] = c

    get = lambda x, y: u_ref[x, y]
    (far_lo, near_lo), (near_hi, far_hi) = [[layer(ref, i, parts, ny, np_) for i in (0, 1)] for ref in (lo_ref, hi_ref)]
    for old, new in ((v_in, v_ref), (dn_in, dn_ref), (up_in, up_ref)):
        new[1 : nx - 1] = old[1 : nx - 1]
    _, put = split(ny, dn_ref, v_ref, up_ref)
    sweep(nx, ny, nz, range(ny), get, c_ref, near_lo, near_hi, None, put, None, (0, nx - 1))

    def beyond(side, row, before, after, out_ref):
        def emit(y, total):
            out_ref[y] = total

        column(ny, nz, range(ny), row, before, after, lambda i, y: k_ref[side, i, pl.ds(y, 1), :], None, emit)

    beyond(0, near_lo, far_lo, lambda y: get(0, y), vlo_ref)
    beyond(1, near_hi, lambda y: get(nx - 1, y), far_hi, vhi_ref)


def close_kernel(nx, ny, np_, c_ref, below_ref, above_ref, dn_ref, up_ref, low_ref, high_ref, xlo_ref, xhi_ref):
    last = ny - 1
    for x in range(nx):
        rows = slice(x * np_, (x + 1) * np_)
        low = c_ref[YM, x, 0:1, :] * below_ref[rows, :]
        high = c_ref[YP, x, last : last + 1, :] * above_ref[rows, :]
        low_ref[x] = dn_ref[x] + low
        high_ref[x] = up_ref[x] + high
        if x == 0:
            xlo_ref[0], xlo_ref[1] = low, high
        if x == nx - 1:
            xhi_ref[0], xhi_ref[1] = low, high


def pieces(a):
    high = a.astype(BF16)
    rest = a - high.astype(F32)
    mid = rest.astype(BF16)
    return high, mid, (rest - mid.astype(F32)).astype(BF16)


def square(a):
    stack = jnp.concatenate(pieces(a), axis=0)
    return lax.dot_general(stack, stack, (((1,), (1,)), ((), ())), preferred_element_type=F32)


def fold(n, a):
    block = lambda i, j: a[i * n : i * n + n, j * n : j * n + n]
    return block(0, 0) + ((block(0, 1) + block(1, 0)) + (block(1, 1) + (block(0, 2) + block(2, 0))))


def border_kernel(
    nx, ny, np_, nz, up_ref, dn_ref, v_ref, vlow_ref, vhigh_ref, c_ref, below_ref, above_ref, lo_ref, hi_ref,
    w_ref, wends_ref, wlow_ref, whigh_ref, g_ref,
):
    half = nx * np_
    get, _ = split(ny, vlow_ref, v_ref, vhigh_ref)

    def ring(x, y):
        side, own = (below_ref, dn_ref) if y == 0 else (above_ref, up_ref)
        return side[pl.ds(half + x, 1), :] * own[pl.ds(x * np_, np_), :]

    g_ref[...] = jnp.zeros_like(g_ref)

    def emit(x, y, total):
        if y == 0:
            wlow_ref[x] = total
        elif y == ny - 1:
            whigh_ref[x] = total
        else:
            w_ref[x, 0 if y == 1 else 1] = total
            g_ref[...] += square(total)

    ends = (0, 1, nx - 2, nx - 1)

    def emit_ends(x, y, total):
        wends_ref[ends.index(x), y - 2] = total
        g_ref[...] += square(total)

    lo, hi = face(lo_ref), face(hi_ref)
    sweep(nx, ny, nz, (0, 1, ny - 2, ny - 1), get, c_ref, lo, hi, ring, emit, (1, nx - 1), (0, nx - 1))
    sweep(nx, ny, nz, range(2, ny - 2), get, c_ref, lo, hi, None, emit_ends, None, ends)


def last_kernel(
    nx, ny, np_, copies, c_ref, below_ref, above_ref, lo_ref, hi_ref, ga_ref, gb_ref, wlow_in, whigh_in,
    wlow_ref, whigh_ref, g_ref,
):
    last = ny - 1
    gram = ga_ref[...] + gb_ref[...]
    for x in range(nx):
        low = wlow_in[x] + c_ref[YM, x, 0:1, :] * below_ref[x]
        high = whigh_in[x] + c_ref[YP, x, last : last + 1, :] * above_ref[x]
        if x == 0:
            low = low + c_ref[XM, x, 0:1, :] * lo_ref[0]
            high = high + c_ref[XM, x, last : last + 1, :] * lo_ref[1]
        if x == nx - 1:
            low = low + c_ref[XP, x, 0:1, :] * hi_ref[0]
            high = high + c_ref[XP, x, last : last + 1, :] * hi_ref[1]
        wlow_ref[x] = low
        whigh_ref[x] = high
        gram = gram + (square(low) + square(high))
    gram = fold(np_, gram)
    packed = jnp.concatenate([gram[8 * i : 8 * i + 8, :] for i in range(np_ // 8)], axis=1)
    for i in range(copies):
        g_ref[i] = packed


def factor_and_inverse(n, gram, factor_ref, inv_ref):
    eye = lax.broadcasted_iota(jnp.int32, (n, n), 0) == lax.broadcasted_iota(jnp.int32, (n, n), 1)
    a = jnp.concatenate([gram, jnp.where(eye, 1.0, 0.0)], axis=1)
    sub = lax.broadcasted_iota(jnp.int32, (n, 2 * n), 0)
    lane = lax.broadcasted_iota(jnp.int32, (1, n), 1)
    for k0 in range(0, n, BLOCK):
        cols = [jnp.broadcast_to(a[k0:, k : k + 1], (n - k0, 2 * n)) for k in range(k0, k0 + BLOCK)]
        low, rows = a[k0:], sub[k0:]
        for j in range(BLOCK):
            k = k0 + j
            r = lax.rsqrt(cols[j][j : j + 1, :])
            row = low[j : j + 1, :] * r
            factor_ref[k : k + 1, :] = jnp.where(lane >= k, row[:, :n], 0.0)
            inv_ref[k : k + 1, :] = row[:, n:]
            col = jnp.where(rows > k, cols[j] * r, 0.0)
            for m in range(j + 1, BLOCK):
                cols[m] = cols[m] - col * (cols[m][j : j + 1, :] * r)
            low = low - col * row
        a = low if k0 == 0 else jnp.concatenate([a[:k0], low], axis=0)


def basis_kernel(
    nx, ny, np_, scale, g_ref, w_ref, wside_ref, wends_ref, wlow_ref, whigh_ref, out_ref, factor_ref, inv_ref, stage, sems
):
    def get(x, y):
        if y in (0, ny - 1):
            return wlow_ref[x] if y == 0 else whigh_ref[x]
        if y in (1, ny - 2):
            return wside_ref[x, 0 if y == 1 else 1]
        ends = (0, 1, nx - 2, nx - 1)
        return wends_ref[ends.index(x), y - 2] if x in ends else w_ref[x - 2, y - 2]

    n = np_
    total = jnp.sum(g_ref[...], axis=0) * scale
    gram = jnp.concatenate([total[:, n * i : n * i + n] for i in range(n // 8)], axis=0)
    factor_and_inverse(n, gram, factor_ref, inv_ref)
    high, mid, low = pieces(inv_ref[...])
    none = jnp.zeros_like(high)
    left = jnp.concatenate(
        [jnp.concatenate(row, axis=1) for row in ((high, high, high), (mid, mid, none), (low, none, none))], axis=0
    )
    parts = wlow_ref.shape[2] // LANES
    group = parts * ny
    copies = []
    for x in range(nx):
        for y in range(ny):
            right = jnp.concatenate(pieces(get(x, y)), axis=0)
            terms = lax.dot_general(left, right, (((1,), (0,)), ((), ())), preferred_element_type=F32)
            block = terms[:n] + (terms[n : 2 * n] + terms[2 * n :])
            for h in range(parts):
                stage.at[x][pl.ds(h * ny + y, n, stride=group), :] = block[:, h * LANES : (h + 1) * LANES]
        copy = pltpu.make_async_copy(stage.at[x].reshape(n, group, LANES), out_ref.at[:, x], sems.at[x])
        copy.start()
        copies.append(copy)
    for copy in copies:
        copy.wait()


def on_device(probes, diffusion, velocity):
    np_, nx, ny, nz = probes.shape
    mx, my = lax.axis_size("gx"), lax.axis_size("gy")
    cells = mx * my * nx * ny * nz
    grid = (nx, ny, np_, nz)
    corner = (2, np_, nz)
    square_sum = (3 * np_, 3 * np_)
    plane = (nx, np_, nz)
    face_shape = (ny, np_, nz)
    tall = (nx * np_ + nx, nz)
    up_x = [(i, i + 1) for i in range(mx - 1)]
    dn_x = [(i + 1, i) for i in range(mx - 1)]
    up_y = [(i, i + 1) for i in range(my - 1)]
    dn_y = [(i + 1, i) for i in range(my - 1)]

    parts = nz // LANES
    tiled = lambda a: jnp.swapaxes(a.reshape(a.shape[:-1] + (parts, LANES)), -2, -3)
    tiles = tiled(probes)
    wide = ((2 * np_ + 4) * parts * ny, LANES)
    hbm = pl.BlockSpec(memory_space=pltpu.HBM)
    operands = [tiles, tiled(diffusion), tiled(velocity)]
    up, dn = call(
        functools.partial(edge_kernel, nx, ny, np_, parts),
        [tall, tall],
        operands,
        scratch=[pltpu.VMEM((4, nx, nz), F32), pltpu.SemaphoreType.DMA],
        in_specs=[hbm] * 3,
        name="edge",
        vmem=61,
    )
    below = lax.ppermute(up, "gy", up_y)
    above = lax.ppermute(dn, "gy", dn_y)
    some = (nx, ny - 2, np_, nz)
    shapes = [some, plane, plane, face_shape, face_shape, (nx - 4, ny - 4, np_, nz), square_sum]

    def inside(tiles, diffusion, velocity):
        xlo, xhi = call(
            functools.partial(side_kernel, nx, ny, np_, parts),
            [wide, wide],
            [tiles, tiled(diffusion), tiled(velocity)],
            scratch=[pltpu.SemaphoreType.DMA],
            in_specs=[hbm] * 3,
            name="side",
        )
        before = lax.ppermute(xhi, "gx", up_x)
        after = lax.ppermute(xlo, "gx", dn_x)
        u, coef, v, dn2, up2, w, gram = call(
            functools.partial(first_kernel, nx, ny, np_, nz),
            [grid, (7, nx, ny, nz), some, plane, plane, *shapes[5:]],
            [tiles.reshape(-1, LANES), diffusion, velocity],
            name="first",
        )
        made = call(
            functools.partial(outer_kernel, nx, ny, np_, nz),
            shapes[:5],
            [u, coef, before, after, v, dn2, up2],
            scratch=[pltpu.VMEM((2, 7, ny, nz), F32)],
            name="outer",
        )
        return (*made, w, gram)

    def outside(*_):
        return tuple(jnp.zeros(shape, F32) for shape in shapes)

    always = lax.axis_index("gx") >= 0
    v, dn2, up2, vlo, vhi, w, gram = lax.cond(always, inside, outside, tiles, diffusion, velocity)
    below2 = lax.ppermute(up2, "gy", up_y)
    above2 = lax.ppermute(dn2, "gy", dn_y)
    (coef,) = call(coefficient_kernel, [(7, nx, ny, nz)], [diffusion, velocity], name="coef")
    vlow, vhigh, xlo3, xhi3 = call(
        functools.partial(close_kernel, nx, ny, np_),
        [plane, plane, corner, corner],
        [coef, below, above, dn2, up2],
        name="close",
    )
    before3 = lax.ppermute(xhi3, "gx", up_x)
    after3 = lax.ppermute(xlo3, "gx", dn_x)
    wside, wends, wlow, whigh, gram2 = call(
        functools.partial(border_kernel, nx, ny, np_, nz),
        [(nx, 2, np_, nz), (4, ny - 4, np_, nz), plane, plane, square_sum],
        [up, dn, v, vlow, vhigh, coef, below, above, vlo, vhi],
        name="border",
    )
    wlow, whigh, grams = call(
        functools.partial(last_kernel, nx, ny, np_, mx * my),
        [plane, plane, (mx * my, 8, np_ * np_ // 8)],
        [coef, below2, above2, before3, after3, gram, gram2, wlow, whigh],
        name="last",
    )
    grams = lax.all_to_all(grams, ("gx", "gy"), 0, 0, tiled=True)
    basis, factor = call(
        functools.partial(basis_kernel, nx, ny, np_, 1.0 / cells),
        [(np_, nx, parts * ny, LANES), (np_, np_)],
        [grams, w, wside, wends, wlow, whigh],
        scratch=[
            pltpu.VMEM((np_, np_), F32),
            pltpu.VMEM((nx, np_ * parts * ny, LANES), F32),
            pltpu.SemaphoreType.DMA((nx,)),
        ],
        out_specs=[ANY, VMEM],
        name="basis",
    )
    basis = basis.reshape(np_, nx, parts, ny, LANES).transpose(0, 1, 3, 2, 4).reshape(np_, nx, ny, nz)
    return basis, factor


def solution(mesh):
    return jax.shard_map(
        on_device,
        mesh=mesh,
        in_specs=(P(None, "gx", "gy", None), P("gx", "gy", None), P(None, "gx", "gy", None)),
        out_specs=(P(None, "gx", "gy", None), P()),
        check_vma=False,
    )
```

```python
import functools

import jax
import jax.numpy as jnp
from jax import lax
from jax.experimental import pallas as pl
from jax.experimental.pallas import tpu as pltpu
from jax.sharding import PartitionSpec as P

F32 = jnp.float32
BF16 = jnp.bfloat16
VMEM = pl.BlockSpec(memory_space=pltpu.VMEM)
ANY = pl.BlockSpec(memory_space=pl.ANY)
LANES = 128
BLOCK = 16
W0, XP, XM, YP, YM, ZP, ZM = range(7)


def call(body, outs, ins, scratch=(), in_specs=None, out_specs=None, name=None, vmem=24, aliases=None):
    return pl.pallas_call(
        body,
        out_shape=[jax.ShapeDtypeStruct(s, F32) for s in outs],
        in_specs=in_specs or [VMEM] * len(ins),
        out_specs=out_specs or [VMEM] * len(outs),
        scratch_shapes=list(scratch),
        input_output_aliases=aliases or {},
        compiler_params=pltpu.CompilerParams(vmem_limit_bytes=vmem << 20),
        name=name,
    )(*ins)


def even(axis):
    return lax.rem(lax.axis_index(axis), 2) == 0


def swaps(count):
    pairs = [[(i, i + 1) for i in range(first, count - 1, 2)] for first in (0, 1)]
    return [[(i, j) for pair in each for i, j in (pair, pair[::-1])] for each in pairs]


def exchange(one, two, axis):
    first, second = swaps(lax.axis_size(axis))
    return lax.ppermute(one, axis, first), lax.ppermute(two, axis, second)


def sides(is_even, one, two):
    low = lambda *at: jnp.where(is_even, two[at], one[at])
    high = lambda *at: jnp.where(is_even, one[at], two[at])
    return low, high


def move(pairs, sem):
    copies = [pltpu.make_async_copy(src, dst, sem) for src, dst in pairs]
    for copy in copies:
        copy.start()
    for copy in copies:
        copy.wait()


def edge_kernel(nx, ny, np_, parts, p_ref, d_ref, v_ref, one_ref, two_ref, terms, sem):
    last = ny - 1
    half = nx * np_

    def fill(up_ref, dn_ref):
        copies = []
        for x in range(nx):
            rows = pl.ds(x * np_, np_)
            for h in range(parts):
                lanes = pl.ds(h * LANES, LANES)
                copies.append((p_ref.at[:, x, h, last, :], up_ref.at[rows, lanes]))
                copies.append((p_ref.at[:, x, h, 0, :], dn_ref.at[rows, lanes]))
        for h in range(parts):
            for i, y in enumerate((0, last)):
                copies.append((d_ref.at[:, h, y, :], terms.at[i, :, pl.ds(h * LANES, LANES)]))
                copies.append((v_ref.at[1, :, h, y, :], terms.at[2 + i, :, pl.ds(h * LANES, LANES)]))
        move(copies, sem)
        dn_ref[half : half + nx, :] = terms[0] + 0.5 * terms[2]
        up_ref[half : half + nx, :] = terms[1] - 0.5 * terms[3]

    is_even = even("gy")

    @pl.when(is_even)
    def _():
        fill(one_ref, two_ref)

    @pl.when(jnp.logical_not(is_even))
    def _():
        fill(two_ref, one_ref)


def side_kernel(nx, ny, np_, parts, p_ref, d_ref, v_ref, one_ref, two_ref, sem):
    layers = np_ * 2 * parts * ny
    some = parts * ny

    def fill(hi_ref, lo_ref):
        copies = []
        for ref, first, outer in ((lo_ref, 0, 0), (hi_ref, nx - 2, nx - 1)):
            copies.append((p_ref.at[:, pl.ds(first, 2)], ref.at[pl.ds(0, layers)].reshape(np_, 2, parts, ny, LANES)))
            copies.append((d_ref.at[outer], ref.at[pl.ds(layers, some)].reshape(parts, ny, LANES)))
            copies.append((v_ref.at[:, outer], ref.at[pl.ds(layers + some, 3 * some)].reshape(3, parts, ny, LANES)))
        move(copies, sem)

    is_even = even("gx")

    @pl.when(is_even)
    def _():
        fill(one_ref, two_ref)

    @pl.when(jnp.logical_not(is_even))
    def _():
        fill(two_ref, one_ref)


def coefficients(d, vx, vy, vz):
    z = lax.broadcasted_iota(jnp.int32, d.shape, d.ndim - 1)
    return (
        1.0 - 6.0 * d,
        d - 0.5 * vx,
        d + 0.5 * vx,
        d - 0.5 * vy,
        d + 0.5 * vy,
        jnp.where(z == d.shape[-1] - 1, 0.0, d - 0.5 * vz),
        jnp.where(z == 0, 0.0, d + 0.5 * vz),
    )


def spread(nx, ny, np_, parts, p_ref, u_ref):
    for x in range(nx):
        for y in range(ny):
            for h in range(parts):
                block = p_ref[pl.ds((x * parts + h) * ny + y, np_, stride=nx * parts * ny), :]
                u_ref[x, y, :, h * LANES : (h + 1) * LANES] = block


def coefficient_kernel(d_ref, v_ref, c_ref):
    for i, c in enumerate(coefficients(d_ref[...], v_ref[0], v_ref[1], v_ref[2])):
        c_ref[i] = c


def column(ny, nz, ys, row, before, after, coef, ring, emit):
    rows = {y: row(y) for y in sorted({n for y in ys for n in (y - 1, y, y + 1) if 0 <= n < ny})}
    for y in ys:
        here = rows[y]
        k = lambda i: coef(i, y)
        total = k(W0) * here
        total = total + k(XP) * after(y) + k(XM) * before(y)
        if y + 1 < ny:
            total = total + k(YP) * rows[y + 1]
        elif ring is not None:
            total = total + k(YP) * ring(y)
        if y > 0:
            total = total + k(YM) * rows[y - 1]
        elif ring is not None:
            total = total + k(YM) * ring(y)
        total = total + k(ZP) * pltpu.roll(here, nz - 1, 1) + k(ZM) * pltpu.roll(here, 1, 1)
        emit(y, total)


def sweep(nx, ny, nz, ys, get, c_ref, lo, hi, ring, emit, loop=None, ends=None):
    def at(x, before, after):
        outside = None if ring is None else lambda y: ring(x, y)
        coef = lambda i, y: c_ref[i, x, pl.ds(y, 1), :]
        column(ny, nz, ys, lambda y: get(x, y), before, after, coef, outside, lambda y, total: emit(x, y, total))

    for x in ends:
        at(x, lo if x == 0 else lambda y: get(x - 1, y), hi if x == nx - 1 else lambda y: get(x + 1, y))
    if loop is not None:

        @pl.loop(*loop)
        def _(x):
            at(x, lambda y: get(x - 1, y), lambda y: get(x + 1, y))


def split(ny, low, inner, high):
    def get(x, y):
        return low[x] if y == 0 else high[x] if y == ny - 1 else inner[x, y - 1]

    def put(x, y, value):
        if y == 0:
            low[x] = value
        elif y == ny - 1:
            high[x] = value
        else:
            inner[x, y - 1] = value

    return get, put


def layer(rows, i, parts, ny, np_):
    def get(y):
        each = [rows(pl.ds((i * parts + h) * ny + y, np_, stride=2 * parts * ny), slice(None)) for h in range(parts)]
        return jnp.concatenate(each, axis=1)

    return get


def face(ref):
    return lambda y: ref[y]


def first_kernel(nx, ny, np_, nz, p_ref, d_ref, v_ref, u_ref, c_ref, out_ref, dn_ref, up_ref, w_ref, g_ref):
    spread(nx, ny, np_, nz // LANES, p_ref, u_ref)
    coefficient_kernel(d_ref, v_ref, c_ref)
    get, put = split(ny, dn_ref, out_ref, up_ref)
    sweep(nx, ny, nz, range(ny), lambda x, y: u_ref[x, y], c_ref, None, None, None, put, (1, nx - 1), ())
    g_ref[...] = jnp.zeros_like(g_ref)

    def emit(x, y, total):
        w_ref[x - 2, y - 2] = total
        g_ref[...] += square(total)

    sweep(nx, ny, nz, range(2, ny - 2), get, c_ref, None, None, None, emit, (2, nx - 2), ())


def outer_kernel(
    nx, ny, np_, nz, u_ref, c_ref, xone_ref, xtwo_ref, v_in, dn_in, up_in,
    v_ref, one_ref, two_ref, vlo_ref, vhi_ref, k_ref, dn_ends, up_ends,
):
    parts = nz // LANES
    layers = np_ * 2 * parts * ny
    messages = sides(even("gx"), xone_ref, xtwo_ref)
    for side, rows in enumerate(messages):
        tile = lambda i: jnp.concatenate(
            [rows(pl.ds(layers + (i * parts + h) * ny, ny), slice(None)) for h in range(parts)], axis=1
        )
        for i, c in enumerate(coefficients(tile(0), tile(1), tile(2), tile(3))):
            k_ref[side, i] = c

    get = lambda x, y: u_ref[x, y]
    (far_lo, near_lo), (near_hi, far_hi) = [[layer(rows, i, parts, ny, np_) for i in (0, 1)] for rows in messages]
    v_ref[1 : nx - 1] = v_in[1 : nx - 1]
    ends = {0: 0, nx - 1: 1}

    def put(x, y, total):
        if y == 0:
            dn_ends[ends[x]] = total
        elif y == ny - 1:
            up_ends[ends[x]] = total
        else:
            v_ref[x, y - 1] = total

    sweep(nx, ny, nz, range(ny), get, c_ref, near_lo, near_hi, None, put, None, (0, nx - 1))
    is_even = even("gy")
    for x in range(nx):
        dn, up = (dn_ends[ends[x]], up_ends[ends[x]]) if x in ends else (dn_in[x], up_in[x])
        one_ref[x] = jnp.where(is_even, up, dn)
        two_ref[x] = jnp.where(is_even, dn, up)

    def beyond(side, row, before, after, out_ref):
        def emit(y, total):
            out_ref[y] = total

        column(ny, nz, range(ny), row, before, after, lambda i, y: k_ref[side, i, pl.ds(y, 1), :], None, emit)

    beyond(0, near_lo, far_lo, lambda y: get(0, y), vlo_ref)
    beyond(1, near_hi, lambda y: get(nx - 1, y), far_hi, vhi_ref)


def close_kernel(
    nx, ny, np_, c_ref, rone_ref, rtwo_ref, one_ref, two_ref, low_ref, high_ref, xone_ref, xtwo_ref
):
    last = ny - 1
    below, above = sides(even("gy"), rone_ref, rtwo_ref)
    dn, up = sides(even("gy"), one_ref, two_ref)
    ends = {}
    for x in range(nx):
        rows = slice(x * np_, (x + 1) * np_)
        low = c_ref[YM, x, 0:1, :] * below(rows, slice(None))
        high = c_ref[YP, x, last : last + 1, :] * above(rows, slice(None))
        low_ref[x] = dn(x) + low
        high_ref[x] = up(x) + high
        ends[x] = low, high
    is_even = even("gx")
    for i in range(2):
        lo, hi = ends[0][i], ends[nx - 1][i]
        xone_ref[i] = jnp.where(is_even, hi, lo)
        xtwo_ref[i] = jnp.where(is_even, lo, hi)


def pieces(a):
    high = a.astype(BF16)
    rest = a - high.astype(F32)
    mid = rest.astype(BF16)
    return high, mid, (rest - mid.astype(F32)).astype(BF16)


def square(a):
    stack = jnp.concatenate(pieces(a), axis=0)
    return lax.dot_general(stack, stack, (((1,), (1,)), ((), ())), preferred_element_type=F32)


def fold(n, a):
    block = lambda i, j: a[i * n : i * n + n, j * n : j * n + n]
    return block(0, 0) + ((block(0, 1) + block(1, 0)) + (block(1, 1) + (block(0, 2) + block(2, 0))))


def border_kernel(
    nx, ny, np_, nz, one_ref, two_ref, v_ref, vlow_ref, vhigh_ref, c_ref, rone_ref, rtwo_ref, lo_ref, hi_ref,
    w_ref, wends_ref, wlow_ref, whigh_ref, g_ref,
):
    half = nx * np_
    get, _ = split(ny, vlow_ref, v_ref, vhigh_ref)

    received = sides(even("gy"), rone_ref, rtwo_ref)
    sent = sides(even("gy"), one_ref, two_ref)

    def ring(x, y):
        side, all_z = 0 if y == 0 else 1, slice(None)
        return received[side](pl.ds(half + x, 1), all_z) * sent[side](pl.ds(x * np_, np_), all_z)

    g_ref[...] = jnp.zeros_like(g_ref)

    def emit(x, y, total):
        if y == 0:
            wlow_ref[x] = total
        elif y == ny - 1:
            whigh_ref[x] = total
        else:
            w_ref[x, 0 if y == 1 else 1] = total
            g_ref[...] += square(total)

    ends = (0, 1, nx - 2, nx - 1)

    def emit_ends(x, y, total):
        wends_ref[ends.index(x), y - 2] = total
        g_ref[...] += square(total)

    lo, hi = face(lo_ref), face(hi_ref)
    sweep(nx, ny, nz, (0, 1, ny - 2, ny - 1), get, c_ref, lo, hi, ring, emit, (1, nx - 1), (0, nx - 1))
    sweep(nx, ny, nz, range(2, ny - 2), get, c_ref, lo, hi, None, emit_ends, None, ends)


def last_kernel(
    nx, ny, np_, copies, c_ref, rone_ref, rtwo_ref, xone_ref, xtwo_ref, ga_ref, gb_ref, wlow_in, whigh_in,
    wlow_ref, whigh_ref, g_ref,
):
    last = ny - 1
    gram = ga_ref[...] + gb_ref[...]
    below, above = sides(even("gy"), rone_ref, rtwo_ref)
    before, after = sides(even("gx"), xone_ref, xtwo_ref)
    for x in range(nx):
        low = wlow_in[x] + c_ref[YM, x, 0:1, :] * below(x)
        high = whigh_in[x] + c_ref[YP, x, last : last + 1, :] * above(x)
        if x == 0:
            low = low + c_ref[XM, x, 0:1, :] * before(0)
            high = high + c_ref[XM, x, last : last + 1, :] * before(1)
        if x == nx - 1:
            low = low + c_ref[XP, x, 0:1, :] * after(0)
            high = high + c_ref[XP, x, last : last + 1, :] * after(1)
        wlow_ref[x] = low
        whigh_ref[x] = high
        gram = gram + (square(low) + square(high))
    gram = fold(np_, gram)
    packed = jnp.concatenate([gram[8 * i : 8 * i + 8, :] for i in range(np_ // 8)], axis=1)
    for i in range(copies):
        g_ref[i] = packed


def factor_and_inverse(n, gram, factor_ref, inv_ref):
    eye = lax.broadcasted_iota(jnp.int32, (n, n), 0) == lax.broadcasted_iota(jnp.int32, (n, n), 1)
    a = jnp.concatenate([gram, jnp.where(eye, 1.0, 0.0)], axis=1)
    sub = lax.broadcasted_iota(jnp.int32, (n, 2 * n), 0)
    lane = lax.broadcasted_iota(jnp.int32, (1, n), 1)
    for k0 in range(0, n, BLOCK):
        cols = [jnp.broadcast_to(a[k0:, k : k + 1], (n - k0, 2 * n)) for k in range(k0, k0 + BLOCK)]
        low, rows = a[k0:], sub[k0:]
        for j in range(BLOCK):
            k = k0 + j
            r = lax.rsqrt(cols[j][j : j + 1, :])
            row = low[j : j + 1, :] * r
            factor_ref[k : k + 1, :] = jnp.where(lane >= k, row[:, :n], 0.0)
            inv_ref[k : k + 1, :] = row[:, n:]
            col = jnp.where(rows > k, cols[j] * r, 0.0)
            for m in range(j + 1, BLOCK):
                cols[m] = cols[m] - col * (cols[m][j : j + 1, :] * r)
            low = low - col * row
        a = low if k0 == 0 else jnp.concatenate([a[:k0], low], axis=0)


def basis_kernel(
    nx, ny, np_, scale, g_ref, w_ref, wside_ref, wends_ref, wlow_ref, whigh_ref, out_ref, factor_ref, inv_ref, stage, sems
):
    def get(x, y):
        if y in (0, ny - 1):
            return wlow_ref[x] if y == 0 else whigh_ref[x]
        if y in (1, ny - 2):
            return wside_ref[x, 0 if y == 1 else 1]
        ends = (0, 1, nx - 2, nx - 1)
        return wends_ref[ends.index(x), y - 2] if x in ends else w_ref[x - 2, y - 2]

    n = np_
    total = jnp.sum(g_ref[...], axis=0) * scale
    gram = jnp.concatenate([total[:, n * i : n * i + n] for i in range(n // 8)], axis=0)
    factor_and_inverse(n, gram, factor_ref, inv_ref)
    high, mid, low = pieces(inv_ref[...])
    none = jnp.zeros_like(high)
    left = jnp.concatenate(
        [jnp.concatenate(row, axis=1) for row in ((high, high, high), (mid, mid, none), (low, none, none))], axis=0
    )
    parts = wlow_ref.shape[2] // LANES
    group = parts * ny
    copies = []
    for x in range(nx):
        for y in range(ny):
            right = jnp.concatenate(pieces(get(x, y)), axis=0)
            terms = lax.dot_general(left, right, (((1,), (0,)), ((), ())), preferred_element_type=F32)
            block = terms[:n] + (terms[n : 2 * n] + terms[2 * n :])
            for h in range(parts):
                stage.at[x][pl.ds(h * ny + y, n, stride=group), :] = block[:, h * LANES : (h + 1) * LANES]
        copy = pltpu.make_async_copy(stage.at[x].reshape(n, group, LANES), out_ref.at[:, x], sems.at[x])
        copy.start()
        copies.append(copy)
    for copy in copies:
        copy.wait()


def on_device(probes, diffusion, velocity):
    np_, nx, ny, nz = probes.shape
    mx, my = lax.axis_size("gx"), lax.axis_size("gy")
    cells = mx * my * nx * ny * nz
    grid = (nx, ny, np_, nz)
    corner = (2, np_, nz)
    square_sum = (3 * np_, 3 * np_)
    plane = (nx, np_, nz)
    face_shape = (ny, np_, nz)
    tall = (nx * np_ + nx, nz)
    parts = nz // LANES
    tiled = lambda a: jnp.swapaxes(a.reshape(a.shape[:-1] + (parts, LANES)), -2, -3)
    tiles = tiled(probes)
    wide = ((2 * np_ + 4) * parts * ny, LANES)
    hbm = pl.BlockSpec(memory_space=pltpu.HBM)
    operands = [tiles, tiled(diffusion), tiled(velocity)]
    one, two = call(
        functools.partial(edge_kernel, nx, ny, np_, parts),
        [tall, tall],
        operands,
        scratch=[pltpu.VMEM((4, nx, nz), F32), pltpu.SemaphoreType.DMA],
        in_specs=[hbm] * 3,
        name="edge",
        vmem=61,
    )
    rone, rtwo = exchange(one, two, "gy")
    some = (nx, ny - 2, np_, nz)
    shapes = [some, plane, plane, face_shape, face_shape, (nx - 4, ny - 4, np_, nz), square_sum]

    def inside(tiles, diffusion, velocity):
        xone, xtwo = call(
            functools.partial(side_kernel, nx, ny, np_, parts),
            [wide, wide],
            [tiles, tiled(diffusion), tiled(velocity)],
            scratch=[pltpu.SemaphoreType.DMA],
            in_specs=[hbm] * 3,
            name="side",
        )
        xone, xtwo = exchange(xone, xtwo, "gx")
        u, coef, v, dn2, up2, w, gram = call(
            functools.partial(first_kernel, nx, ny, np_, nz),
            [grid, (7, nx, ny, nz), some, plane, plane, *shapes[5:]],
            [tiles.reshape(-1, LANES), diffusion, velocity],
            name="first",
        )
        made = call(
            functools.partial(outer_kernel, nx, ny, np_, nz),
            shapes[:5],
            [u, coef, xone, xtwo, v, dn2, up2],
            scratch=[pltpu.VMEM((2, 7, ny, nz), F32), pltpu.VMEM((2, np_, nz), F32), pltpu.VMEM((2, np_, nz), F32)],
            name="outer",
        )
        return (*made, w, gram)

    def outside(*_):
        return tuple(jnp.zeros(shape, F32) for shape in shapes)

    always = lax.axis_index("gx") >= 0
    v, one2, two2, vlo, vhi, w, gram = lax.cond(always, inside, outside, tiles, diffusion, velocity)
    rone2, rtwo2 = exchange(one2, two2, "gy")
    (coef,) = call(coefficient_kernel, [(7, nx, ny, nz)], [diffusion, velocity], name="coef")
    vlow, vhigh, xone3, xtwo3 = call(
        functools.partial(close_kernel, nx, ny, np_),
        [plane, plane, corner, corner],
        [coef, rone, rtwo, one2, two2],
        name="close",
    )
    xone3, xtwo3 = exchange(xone3, xtwo3, "gx")
    wside, wends, wlow, whigh, gram2 = call(
        functools.partial(border_kernel, nx, ny, np_, nz),
        [(nx, 2, np_, nz), (4, ny - 4, np_, nz), plane, plane, square_sum],
        [one, two, v, vlow, vhigh, coef, rone, rtwo, vlo, vhi],
        name="border",
    )
    wlow, whigh, grams = call(
        functools.partial(last_kernel, nx, ny, np_, mx * my),
        [plane, plane, (mx * my, 8, np_ * np_ // 8)],
        [coef, rone2, rtwo2, xone3, xtwo3, gram, gram2, wlow, whigh],
        name="last",
    )
    grams = lax.all_to_all(grams, ("gx", "gy"), 0, 0, tiled=True)
    basis, factor = call(
        functools.partial(basis_kernel, nx, ny, np_, 1.0 / cells),
        [(np_, nx, parts * ny, LANES), (np_, np_)],
        [grams, w, wside, wends, wlow, whigh],
        scratch=[
            pltpu.VMEM((np_, np_), F32),
            pltpu.VMEM((nx, np_ * parts * ny, LANES), F32),
            pltpu.SemaphoreType.DMA((nx,)),
        ],
        out_specs=[ANY, VMEM],
        name="basis",
    )
    basis = basis.reshape(np_, nx, parts, ny, LANES).transpose(0, 1, 3, 2, 4).reshape(np_, nx, ny, nz)
    return basis, factor


def solution(mesh):
    return jax.shard_map(
        on_device,
        mesh=mesh,
        in_specs=(P(None, "gx", "gy", None), P("gx", "gy", None), P(None, "gx", "gy", None)),
        out_specs=(P(None, "gx", "gy", None), P()),
        check_vma=False,
    )
```

```python
import functools

import jax
import jax.numpy as jnp
from jax import lax
from jax.experimental import pallas as pl
from jax.experimental.pallas import tpu as pltpu
from jax.sharding import PartitionSpec as P

F32 = jnp.float32
BF16 = jnp.bfloat16
VMEM = pl.BlockSpec(memory_space=pltpu.VMEM)
ANY = pl.BlockSpec(memory_space=pl.ANY)
LANES = 128
BLOCK = 16
W0, XP, XM, YP, YM, ZP, ZM = range(7)


def call(body, outs, ins, scratch=(), in_specs=None, out_specs=None, name=None, vmem=24, aliases=None):
    return pl.pallas_call(
        body,
        out_shape=[jax.ShapeDtypeStruct(s, F32) for s in outs],
        in_specs=in_specs or [VMEM] * len(ins),
        out_specs=out_specs or [VMEM] * len(outs),
        scratch_shapes=list(scratch),
        input_output_aliases=aliases or {},
        compiler_params=pltpu.CompilerParams(vmem_limit_bytes=vmem << 20),
        name=name,
    )(*ins)


def even(axis):
    return lax.rem(lax.axis_index(axis), 2) == 0


def swaps(count):
    pairs = [[(i, i + 1) for i in range(first, count - 1, 2)] for first in (0, 1)]
    return [[(i, j) for pair in each for i, j in (pair, pair[::-1])] for each in pairs]


def exchange(one, two, axis):
    first, second = swaps(lax.axis_size(axis))
    return lax.ppermute(one, axis, first), lax.ppermute(two, axis, second)


def sides(is_even, one, two):
    low = lambda *at: jnp.where(is_even, two[at], one[at])
    high = lambda *at: jnp.where(is_even, one[at], two[at])
    return low, high


def move(pairs, sem):
    copies = [pltpu.make_async_copy(src, dst, sem) for src, dst in pairs]
    for copy in copies:
        copy.start()
    for copy in copies:
        copy.wait()


def edge_kernel(nx, ny, np_, parts, p_ref, d_ref, v_ref, one_ref, two_ref, terms, sem):
    last = ny - 1
    half = nx * np_

    def fill(up_ref, dn_ref):
        copies = []
        for x in range(nx):
            rows = pl.ds(x * np_, np_)
            for h in range(parts):
                lanes = pl.ds(h * LANES, LANES)
                copies.append((p_ref.at[:, x, h, last, :], up_ref.at[rows, lanes]))
                copies.append((p_ref.at[:, x, h, 0, :], dn_ref.at[rows, lanes]))
        for h in range(parts):
            for i, y in enumerate((0, last)):
                copies.append((d_ref.at[:, h, y, :], terms.at[i, :, pl.ds(h * LANES, LANES)]))
                copies.append((v_ref.at[1, :, h, y, :], terms.at[2 + i, :, pl.ds(h * LANES, LANES)]))
        move(copies, sem)
        dn_ref[half : half + nx, :] = terms[0] + 0.5 * terms[2]
        up_ref[half : half + nx, :] = terms[1] - 0.5 * terms[3]

    is_even = even("gy")

    @pl.when(is_even)
    def _():
        fill(one_ref, two_ref)

    @pl.when(jnp.logical_not(is_even))
    def _():
        fill(two_ref, one_ref)


def side_kernel(nx, ny, np_, parts, p_ref, d_ref, v_ref, one_ref, two_ref, sem):
    layers = np_ * 2 * parts * ny
    some = parts * ny

    def fill(hi_ref, lo_ref):
        copies = []
        for ref, first, outer in ((lo_ref, 0, 0), (hi_ref, nx - 2, nx - 1)):
            copies.append((p_ref.at[:, pl.ds(first, 2)], ref.at[pl.ds(0, layers)].reshape(np_, 2, parts, ny, LANES)))
            copies.append((d_ref.at[outer], ref.at[pl.ds(layers, some)].reshape(parts, ny, LANES)))
            copies.append((v_ref.at[:, outer], ref.at[pl.ds(layers + some, 3 * some)].reshape(3, parts, ny, LANES)))
        move(copies, sem)

    is_even = even("gx")

    @pl.when(is_even)
    def _():
        fill(one_ref, two_ref)

    @pl.when(jnp.logical_not(is_even))
    def _():
        fill(two_ref, one_ref)


def coefficients(d, vx, vy, vz):
    z = lax.broadcasted_iota(jnp.int32, d.shape, d.ndim - 1)
    return (
        1.0 - 6.0 * d,
        d - 0.5 * vx,
        d + 0.5 * vx,
        d - 0.5 * vy,
        d + 0.5 * vy,
        jnp.where(z == d.shape[-1] - 1, 0.0, d - 0.5 * vz),
        jnp.where(z == 0, 0.0, d + 0.5 * vz),
    )


def spread(nx, ny, np_, parts, p_ref, u_ref):
    for x in range(nx):
        for y in range(ny):
            for h in range(parts):
                block = p_ref[pl.ds((x * parts + h) * ny + y, np_, stride=nx * parts * ny), :]
                u_ref[x, y, :, h * LANES : (h + 1) * LANES] = block


def coefficient_kernel(d_ref, v_ref, c_ref):
    for i, c in enumerate(coefficients(d_ref[...], v_ref[0], v_ref[1], v_ref[2])):
        c_ref[i] = c


def column(ny, nz, ys, row, before, after, coef, ring, emit):
    rows = {y: row(y) for y in sorted({n for y in ys for n in (y - 1, y, y + 1) if 0 <= n < ny})}
    for y in ys:
        here = rows[y]
        k = lambda i: coef(i, y)
        total = k(W0) * here
        total = total + k(XP) * after(y) + k(XM) * before(y)
        if y + 1 < ny:
            total = total + k(YP) * rows[y + 1]
        elif ring is not None:
            total = total + k(YP) * ring(y)
        if y > 0:
            total = total + k(YM) * rows[y - 1]
        elif ring is not None:
            total = total + k(YM) * ring(y)
        total = total + k(ZP) * pltpu.roll(here, nz - 1, 1) + k(ZM) * pltpu.roll(here, 1, 1)
        emit(y, total)


def sweep(nx, ny, nz, ys, get, c_ref, lo, hi, ring, emit, loop=None, ends=None):
    def at(x, before, after):
        outside = None if ring is None else lambda y: ring(x, y)
        coef = lambda i, y: c_ref[i, x, pl.ds(y, 1), :]
        column(ny, nz, ys, lambda y: get(x, y), before, after, coef, outside, lambda y, total: emit(x, y, total))

    for x in ends:
        at(x, lo if x == 0 else lambda y: get(x - 1, y), hi if x == nx - 1 else lambda y: get(x + 1, y))
    if loop is not None:

        @pl.loop(*loop)
        def _(x):
            at(x, lambda y: get(x - 1, y), lambda y: get(x + 1, y))


def split(ny, low, inner, high):
    def get(x, y):
        return low[x] if y == 0 else high[x] if y == ny - 1 else inner[x, y - 1]

    def put(x, y, value):
        if y == 0:
            low[x] = value
        elif y == ny - 1:
            high[x] = value
        else:
            inner[x, y - 1] = value

    return get, put


def layer(rows, i, parts, ny, np_):
    def get(y):
        each = [rows(pl.ds((i * parts + h) * ny + y, np_, stride=2 * parts * ny), slice(None)) for h in range(parts)]
        return jnp.concatenate(each, axis=1)

    return get


def face(ref):
    return lambda y: ref[y]


def first_kernel(nx, ny, np_, nz, p_ref, d_ref, v_ref, u_ref, c_ref, out_ref, dn_ref, up_ref, w_ref, g_ref):
    spread(nx, ny, np_, nz // LANES, p_ref, u_ref)
    coefficient_kernel(d_ref, v_ref, c_ref)
    get, put = split(ny, dn_ref, out_ref, up_ref)
    sweep(nx, ny, nz, range(ny), lambda x, y: u_ref[x, y], c_ref, None, None, None, put, (1, nx - 1), ())
    g_ref[...] = jnp.zeros_like(g_ref)

    def emit(x, y, total):
        w_ref[x - 2, y - 2] = total
        g_ref[...] += square(total)

    sweep(nx, ny, nz, range(2, ny - 2), get, c_ref, None, None, None, emit, (2, nx - 2), ())


def outer_kernel(
    nx, ny, np_, nz, u_ref, c_ref, xone_ref, xtwo_ref, v_in, dn_in, up_in,
    v_ref, one_ref, two_ref, vlo_ref, vhi_ref, k_ref, dn_ends, up_ends,
):
    parts = nz // LANES
    layers = np_ * 2 * parts * ny
    messages = sides(even("gx"), xone_ref, xtwo_ref)
    for side, rows in enumerate(messages):
        tile = lambda i: jnp.concatenate(
            [rows(pl.ds(layers + (i * parts + h) * ny, ny), slice(None)) for h in range(parts)], axis=1
        )
        for i, c in enumerate(coefficients(tile(0), tile(1), tile(2), tile(3))):
            k_ref[side, i] = c

    get = lambda x, y: u_ref[x, y]
    (far_lo, near_lo), (near_hi, far_hi) = [[layer(rows, i, parts, ny, np_) for i in (0, 1)] for rows in messages]
    v_ref[1 : nx - 1] = v_in[1 : nx - 1]
    ends = {0: 0, nx - 1: 1}

    def put(x, y, total):
        if y == 0:
            dn_ends[ends[x]] = total
        elif y == ny - 1:
            up_ends[ends[x]] = total
        else:
            v_ref[x, y - 1] = total

    sweep(nx, ny, nz, range(ny), get, c_ref, near_lo, near_hi, None, put, None, (0, nx - 1))
    is_even = even("gy")
    for x in range(nx):
        dn, up = (dn_ends[ends[x]], up_ends[ends[x]]) if x in ends else (dn_in[x], up_in[x])
        one_ref[x] = jnp.where(is_even, up, dn)
        two_ref[x] = jnp.where(is_even, dn, up)

    def beyond(side, row, before, after, out_ref):
        def emit(y, total):
            out_ref[y] = total

        column(ny, nz, range(ny), row, before, after, lambda i, y: k_ref[side, i, pl.ds(y, 1), :], None, emit)

    beyond(0, near_lo, far_lo, lambda y: get(0, y), vlo_ref)
    beyond(1, near_hi, lambda y: get(nx - 1, y), far_hi, vhi_ref)


def close_kernel(
    nx, ny, np_, c_ref, rone_ref, rtwo_ref, one_ref, two_ref, low_ref, high_ref, xone_ref, xtwo_ref
):
    last = ny - 1
    below, above = sides(even("gy"), rone_ref, rtwo_ref)
    dn, up = sides(even("gy"), one_ref, two_ref)
    ends = {}
    for x in range(nx):
        rows = slice(x * np_, (x + 1) * np_)
        low = c_ref[YM, x, 0:1, :] * below(rows, slice(None))
        high = c_ref[YP, x, last : last + 1, :] * above(rows, slice(None))
        low_ref[x] = dn(x) + low
        high_ref[x] = up(x) + high
        ends[x] = low, high
    is_even = even("gx")
    for i in range(2):
        lo, hi = ends[0][i], ends[nx - 1][i]
        xone_ref[i] = jnp.where(is_even, hi, lo)
        xtwo_ref[i] = jnp.where(is_even, lo, hi)


def pieces(a):
    high = a.astype(BF16)
    rest = a - high.astype(F32)
    mid = rest.astype(BF16)
    return high, mid, (rest - mid.astype(F32)).astype(BF16)


def square(a):
    stack = jnp.concatenate(pieces(a), axis=0)
    return lax.dot_general(stack, stack, (((1,), (1,)), ((), ())), preferred_element_type=F32)


def fold(n, a):
    block = lambda i, j: a[i * n : i * n + n, j * n : j * n + n]
    return block(0, 0) + ((block(0, 1) + block(1, 0)) + (block(1, 1) + (block(0, 2) + block(2, 0))))


def border_kernel(
    nx, ny, np_, nz, one_ref, two_ref, v_ref, vlow_ref, vhigh_ref, c_ref, rone_ref, rtwo_ref, lo_ref, hi_ref,
    w_ref, wends_ref, wlow_ref, whigh_ref, g_ref,
):
    half = nx * np_
    get, _ = split(ny, vlow_ref, v_ref, vhigh_ref)

    received = sides(even("gy"), rone_ref, rtwo_ref)
    sent = sides(even("gy"), one_ref, two_ref)

    def ring(x, y):
        side, all_z = 0 if y == 0 else 1, slice(None)
        return received[side](pl.ds(half + x, 1), all_z) * sent[side](pl.ds(x * np_, np_), all_z)

    g_ref[...] = jnp.zeros_like(g_ref)

    def emit(x, y, total):
        if y == 0:
            wlow_ref[x] = total
        elif y == ny - 1:
            whigh_ref[x] = total
        else:
            w_ref[x, 0 if y == 1 else 1] = total
            g_ref[...] += square(total)

    ends = (0, 1, nx - 2, nx - 1)

    def emit_ends(x, y, total):
        wends_ref[ends.index(x), y - 2] = total
        g_ref[...] += square(total)

    lo, hi = face(lo_ref), face(hi_ref)
    sweep(nx, ny, nz, (0, 1, ny - 2, ny - 1), get, c_ref, lo, hi, ring, emit, (1, nx - 1), (0, nx - 1))
    sweep(nx, ny, nz, range(2, ny - 2), get, c_ref, lo, hi, None, emit_ends, None, ends)


def last_kernel(
    nx, ny, np_, copies, c_ref, rone_ref, rtwo_ref, xone_ref, xtwo_ref, ga_ref, gb_ref, wlow_in, whigh_in,
    wlow_ref, whigh_ref, g_ref,
):
    last = ny - 1
    gram = ga_ref[...] + gb_ref[...]
    below, above = sides(even("gy"), rone_ref, rtwo_ref)
    before, after = sides(even("gx"), xone_ref, xtwo_ref)
    for x in range(nx):
        low = wlow_in[x] + c_ref[YM, x, 0:1, :] * below(x)
        high = whigh_in[x] + c_ref[YP, x, last : last + 1, :] * above(x)
        if x == 0:
            low = low + c_ref[XM, x, 0:1, :] * before(0)
            high = high + c_ref[XM, x, last : last + 1, :] * before(1)
        if x == nx - 1:
            low = low + c_ref[XP, x, 0:1, :] * after(0)
            high = high + c_ref[XP, x, last : last + 1, :] * after(1)
        wlow_ref[x] = low
        whigh_ref[x] = high
        gram = gram + (square(low) + square(high))
    gram = fold(np_, gram)
    packed = jnp.concatenate([gram[8 * i : 8 * i + 8, :] for i in range(np_ // 8)], axis=1)
    for i in range(copies):
        g_ref[i] = packed


def factor_and_inverse(n, gram, factor_ref, inv_ref):
    eye = lax.broadcasted_iota(jnp.int32, (n, n), 0) == lax.broadcasted_iota(jnp.int32, (n, n), 1)
    a = jnp.concatenate([gram, jnp.where(eye, 1.0, 0.0)], axis=1)
    sub = lax.broadcasted_iota(jnp.int32, (n, 2 * n), 0)
    lane = lax.broadcasted_iota(jnp.int32, (1, n), 1)
    for k0 in range(0, n, BLOCK):
        cols = [jnp.broadcast_to(a[k0:, k : k + 1], (n - k0, 2 * n)) for k in range(k0, k0 + BLOCK)]
        low, rows = a[k0:], sub[k0:]
        for j in range(BLOCK):
            k = k0 + j
            r = lax.rsqrt(cols[j][j : j + 1, :])
            row = low[j : j + 1, :] * r
            factor_ref[k : k + 1, :] = jnp.where(lane >= k, row[:, :n], 0.0)
            inv_ref[k : k + 1, :] = row[:, n:]
            col = jnp.where(rows > k, cols[j] * r, 0.0)
            for m in range(j + 1, BLOCK):
                cols[m] = cols[m] - col * (cols[m][j : j + 1, :] * r)
            low = low - col * row
        a = low if k0 == 0 else jnp.concatenate([a[:k0], low], axis=0)


def basis_kernel(
    nx, ny, np_, scale, g_ref, w_ref, wside_ref, wends_ref, wlow_ref, whigh_ref, out_ref, factor_ref, inv_ref, stage, sems
):
    def get(x, y):
        if y in (0, ny - 1):
            return wlow_ref[x] if y == 0 else whigh_ref[x]
        if y in (1, ny - 2):
            return wside_ref[x, 0 if y == 1 else 1]
        ends = (0, 1, nx - 2, nx - 1)
        return wends_ref[ends.index(x), y - 2] if x in ends else w_ref[x - 2, y - 2]

    n = np_
    total = jnp.sum(g_ref[...], axis=0) * scale
    gram = jnp.concatenate([total[:, n * i : n * i + n] for i in range(n // 8)], axis=0)
    factor_and_inverse(n, gram, factor_ref, inv_ref)
    high, mid, low = pieces(inv_ref[...])
    none = jnp.zeros_like(high)
    left = jnp.concatenate(
        [jnp.concatenate(row, axis=1) for row in ((high, high, high), (mid, mid, none), (low, none, none))], axis=0
    )
    parts = wlow_ref.shape[2] // LANES
    group = parts * ny
    copies = []
    for x in range(nx):
        for y in range(ny):
            right = jnp.concatenate(pieces(get(x, y)), axis=0)
            terms = lax.dot_general(left, right, (((1,), (0,)), ((), ())), preferred_element_type=F32)
            block = terms[:n] + (terms[n : 2 * n] + terms[2 * n :])
            for h in range(parts):
                stage.at[x][pl.ds(h * ny + y, n, stride=group), :] = block[:, h * LANES : (h + 1) * LANES]
        copy = pltpu.make_async_copy(stage.at[x].reshape(n, group, LANES), out_ref.at[:, x], sems.at[x])
        copy.start()
        copies.append(copy)
    for copy in copies:
        copy.wait()


def on_device(probes, diffusion, velocity):
    np_, nx, ny, nz = probes.shape
    mx, my = lax.axis_size("gx"), lax.axis_size("gy")
    cells = mx * my * nx * ny * nz
    grid = (nx, ny, np_, nz)
    corner = (2, np_, nz)
    square_sum = (3 * np_, 3 * np_)
    plane = (nx, np_, nz)
    face_shape = (ny, np_, nz)
    tall = (nx * np_ + nx, nz)
    parts = nz // LANES
    tiled = lambda a: jnp.swapaxes(a.reshape(a.shape[:-1] + (parts, LANES)), -2, -3)
    tiles = tiled(probes)
    wide = ((2 * np_ + 4) * parts * ny, LANES)
    hbm = pl.BlockSpec(memory_space=pltpu.HBM)
    operands = [tiles, tiled(diffusion), tiled(velocity)]
    one, two = call(
        functools.partial(edge_kernel, nx, ny, np_, parts),
        [tall, tall],
        operands,
        scratch=[pltpu.VMEM((4, nx, nz), F32), pltpu.SemaphoreType.DMA],
        in_specs=[hbm] * 3,
        name="edge",
        vmem=24,
    )
    rone, rtwo = exchange(one, two, "gy")
    some = (nx, ny - 2, np_, nz)
    shapes = [some, plane, plane, face_shape, face_shape, (nx - 4, ny - 4, np_, nz), square_sum]

    def inside(tiles, diffusion, velocity):
        xone, xtwo = call(
            functools.partial(side_kernel, nx, ny, np_, parts),
            [wide, wide],
            [tiles, tiled(diffusion), tiled(velocity)],
            scratch=[pltpu.SemaphoreType.DMA],
            in_specs=[hbm] * 3,
            name="side",
        )
        xone, xtwo = exchange(xone, xtwo, "gx")
        u, coef, v, dn2, up2, w, gram = call(
            functools.partial(first_kernel, nx, ny, np_, nz),
            [grid, (7, nx, ny, nz), some, plane, plane, *shapes[5:]],
            [tiles.reshape(-1, LANES), diffusion, velocity],
            name="first",
        )
        made = call(
            functools.partial(outer_kernel, nx, ny, np_, nz),
            shapes[:5],
            [u, coef, xone, xtwo, v, dn2, up2],
            scratch=[pltpu.VMEM((2, 7, ny, nz), F32), pltpu.VMEM((2, np_, nz), F32), pltpu.VMEM((2, np_, nz), F32)],
            name="outer",
        )
        return (*made, w, gram)

    def outside(*_):
        return tuple(jnp.zeros(shape, F32) for shape in shapes)

    always = lax.axis_index("gx") >= 0
    v, one2, two2, vlo, vhi, w, gram = lax.cond(always, inside, outside, tiles, diffusion, velocity)
    rone2, rtwo2 = exchange(one2, two2, "gy")
    (coef,) = call(coefficient_kernel, [(7, nx, ny, nz)], [diffusion, velocity], name="coef")
    vlow, vhigh, xone3, xtwo3 = call(
        functools.partial(close_kernel, nx, ny, np_),
        [plane, plane, corner, corner],
        [coef, rone, rtwo, one2, two2],
        name="close",
    )
    xone3, xtwo3 = exchange(xone3, xtwo3, "gx")
    wside, wends, wlow, whigh, gram2 = call(
        functools.partial(border_kernel, nx, ny, np_, nz),
        [(nx, 2, np_, nz), (4, ny - 4, np_, nz), plane, plane, square_sum],
        [one, two, v, vlow, vhigh, coef, rone, rtwo, vlo, vhi],
        name="border",
    )
    wlow, whigh, grams = call(
        functools.partial(last_kernel, nx, ny, np_, mx * my),
        [plane, plane, (mx * my, 8, np_ * np_ // 8)],
        [coef, rone2, rtwo2, xone3, xtwo3, gram, gram2, wlow, whigh],
        name="last",
    )
    grams = lax.all_to_all(grams, ("gx", "gy"), 0, 0, tiled=True)
    basis, factor = call(
        functools.partial(basis_kernel, nx, ny, np_, 1.0 / cells),
        [(np_, nx, parts * ny, LANES), (np_, np_)],
        [grams, w, wside, wends, wlow, whigh],
        scratch=[
            pltpu.VMEM((np_, np_), F32),
            pltpu.VMEM((nx, np_ * parts * ny, LANES), F32),
            pltpu.SemaphoreType.DMA((nx,)),
        ],
        out_specs=[ANY, VMEM],
        name="basis",
    )
    basis = basis.reshape(np_, nx, parts, ny, LANES).transpose(0, 1, 3, 2, 4).reshape(np_, nx, ny, nz)
    return basis, factor


def solution(mesh):
    return jax.shard_map(
        on_device,
        mesh=mesh,
        in_specs=(P(None, "gx", "gy", None), P("gx", "gy", None), P(None, "gx", "gy", None)),
        out_specs=(P(None, "gx", "gy", None), P()),
        check_vma=False,
    )
```

```python
import functools

import jax
import jax.numpy as jnp
from jax import lax
from jax.experimental import pallas as pl
from jax.experimental.pallas import tpu as pltpu
from jax.sharding import PartitionSpec as P

F32 = jnp.float32
BF16 = jnp.bfloat16
VMEM = pl.BlockSpec(memory_space=pltpu.VMEM)
ANY = pl.BlockSpec(memory_space=pl.ANY)
LANES = 128
BLOCK = 16
W0, XP, XM, YP, YM, ZP, ZM = range(7)


def call(body, outs, ins, scratch=(), in_specs=None, out_specs=None, name=None, vmem=24, aliases=None):
    return pl.pallas_call(
        body,
        out_shape=[jax.ShapeDtypeStruct(s, F32) for s in outs],
        in_specs=in_specs or [VMEM] * len(ins),
        out_specs=out_specs or [VMEM] * len(outs),
        scratch_shapes=list(scratch),
        input_output_aliases=aliases or {},
        compiler_params=pltpu.CompilerParams(vmem_limit_bytes=vmem << 20),
        name=name,
    )(*ins)


def even(axis):
    return lax.rem(lax.axis_index(axis), 2) == 0


def swaps(count):
    pairs = [[(i, i + 1) for i in range(first, count - 1, 2)] for first in (0, 1)]
    return [[(i, j) for pair in each for i, j in (pair, pair[::-1])] for each in pairs]


def exchange(one, two, axis):
    first, second = swaps(lax.axis_size(axis))
    return lax.ppermute(one, axis, first), lax.ppermute(two, axis, second)


def sides(is_even, one, two):
    low = lambda *at: jnp.where(is_even, two[at], one[at])
    high = lambda *at: jnp.where(is_even, one[at], two[at])
    return low, high


def move(pairs, sem):
    copies = [pltpu.make_async_copy(src, dst, sem) for src, dst in pairs]
    for copy in copies:
        copy.start()
    for copy in copies:
        copy.wait()


def edge_kernel(nx, ny, np_, parts, upward, p_ref, d_ref, v_ref, out_ref, terms, sem):
    half = nx * np_

    def fill(y, sign):
        copies = []
        for h in range(parts):
            lanes = pl.ds(h * LANES, LANES)
            for x in range(nx):
                copies.append((p_ref.at[:, x, h, y, :], out_ref.at[pl.ds(x * np_, np_), lanes]))
            copies.append((d_ref.at[:, h, y, :], terms.at[0, :, lanes]))
            copies.append((v_ref.at[1, :, h, y, :], terms.at[1, :, lanes]))
        move(copies, sem)
        out_ref[half : half + nx, :] = terms[0] + sign * 0.5 * terms[1]

    is_up = even("gy") == upward

    @pl.when(is_up)
    def _():
        fill(ny - 1, -1.0)

    @pl.when(jnp.logical_not(is_up))
    def _():
        fill(0, 1.0)


def side_kernel(nx, ny, np_, parts, p_ref, d_ref, v_ref, one_ref, two_ref, sem):
    layers = np_ * 2 * parts * ny
    some = parts * ny

    def fill(hi_ref, lo_ref):
        copies = []
        for ref, first, outer in ((lo_ref, 0, 0), (hi_ref, nx - 2, nx - 1)):
            copies.append((p_ref.at[:, pl.ds(first, 2)], ref.at[pl.ds(0, layers)].reshape(np_, 2, parts, ny, LANES)))
            copies.append((d_ref.at[outer], ref.at[pl.ds(layers, some)].reshape(parts, ny, LANES)))
            copies.append((v_ref.at[:, outer], ref.at[pl.ds(layers + some, 3 * some)].reshape(3, parts, ny, LANES)))
        move(copies, sem)

    is_even = even("gx")

    @pl.when(is_even)
    def _():
        fill(one_ref, two_ref)

    @pl.when(jnp.logical_not(is_even))
    def _():
        fill(two_ref, one_ref)


def coefficients(d, vx, vy, vz):
    z = lax.broadcasted_iota(jnp.int32, d.shape, d.ndim - 1)
    return (
        1.0 - 6.0 * d,
        d - 0.5 * vx,
        d + 0.5 * vx,
        d - 0.5 * vy,
        d + 0.5 * vy,
        jnp.where(z == d.shape[-1] - 1, 0.0, d - 0.5 * vz),
        jnp.where(z == 0, 0.0, d + 0.5 * vz),
    )


def spread(nx, ny, np_, parts, p_ref, u_ref):
    for x in range(nx):
        for y in range(ny):
            for h in range(parts):
                block = p_ref[pl.ds((x * parts + h) * ny + y, np_, stride=nx * parts * ny), :]
                u_ref[x, y, :, h * LANES : (h + 1) * LANES] = block


def coefficient_kernel(d_ref, v_ref, c_ref):
    for i, c in enumerate(coefficients(d_ref[...], v_ref[0], v_ref[1], v_ref[2])):
        c_ref[i] = c


def column(ny, nz, ys, row, before, after, coef, ring, emit):
    rows = {y: row(y) for y in sorted({n for y in ys for n in (y - 1, y, y + 1) if 0 <= n < ny})}
    for y in ys:
        here = rows[y]
        k = lambda i: coef(i, y)
        total = k(W0) * here
        total = total + k(XP) * after(y) + k(XM) * before(y)
        if y + 1 < ny:
            total = total + k(YP) * rows[y + 1]
        elif ring is not None:
            total = total + k(YP) * ring(y)
        if y > 0:
            total = total + k(YM) * rows[y - 1]
        elif ring is not None:
            total = total + k(YM) * ring(y)
        total = total + k(ZP) * pltpu.roll(here, nz - 1, 1) + k(ZM) * pltpu.roll(here, 1, 1)
        emit(y, total)


def sweep(nx, ny, nz, ys, get, c_ref, lo, hi, ring, emit, loop=None, ends=None):
    def at(x, before, after):
        outside = None if ring is None else lambda y: ring(x, y)
        coef = lambda i, y: c_ref[i, x, pl.ds(y, 1), :]
        column(ny, nz, ys, lambda y: get(x, y), before, after, coef, outside, lambda y, total: emit(x, y, total))

    for x in ends:
        at(x, lo if x == 0 else lambda y: get(x - 1, y), hi if x == nx - 1 else lambda y: get(x + 1, y))
    if loop is not None:

        @pl.loop(*loop)
        def _(x):
            at(x, lambda y: get(x - 1, y), lambda y: get(x + 1, y))


def split(ny, low, inner, high):
    def get(x, y):
        return low[x] if y == 0 else high[x] if y == ny - 1 else inner[x, y - 1]

    def put(x, y, value):
        if y == 0:
            low[x] = value
        elif y == ny - 1:
            high[x] = value
        else:
            inner[x, y - 1] = value

    return get, put


def layer(rows, i, parts, ny, np_):
    def get(y):
        each = [rows(pl.ds((i * parts + h) * ny + y, np_, stride=2 * parts * ny), slice(None)) for h in range(parts)]
        return jnp.concatenate(each, axis=1)

    return get


def face(ref):
    return lambda y: ref[y]


def first_kernel(nx, ny, np_, nz, p_ref, d_ref, v_ref, u_ref, c_ref, out_ref, dn_ref, up_ref, w_ref, g_ref):
    spread(nx, ny, np_, nz // LANES, p_ref, u_ref)
    coefficient_kernel(d_ref, v_ref, c_ref)
    get, put = split(ny, dn_ref, out_ref, up_ref)
    sweep(nx, ny, nz, range(ny), lambda x, y: u_ref[x, y], c_ref, None, None, None, put, (1, nx - 1), ())
    g_ref[...] = jnp.zeros_like(g_ref)

    def emit(x, y, total):
        w_ref[x - 2, y - 2] = total
        g_ref[...] += square(total)

    sweep(nx, ny, nz, range(2, ny - 2), get, c_ref, None, None, None, emit, (2, nx - 2), ())


def outer_kernel(
    nx, ny, np_, nz, u_ref, c_ref, xone_ref, xtwo_ref, v_in, dn_in, up_in,
    v_ref, one_ref, two_ref, vlo_ref, vhi_ref, k_ref, dn_ends, up_ends,
):
    parts = nz // LANES
    layers = np_ * 2 * parts * ny
    messages = sides(even("gx"), xone_ref, xtwo_ref)
    for side, rows in enumerate(messages):
        tile = lambda i: jnp.concatenate(
            [rows(pl.ds(layers + (i * parts + h) * ny, ny), slice(None)) for h in range(parts)], axis=1
        )
        for i, c in enumerate(coefficients(tile(0), tile(1), tile(2), tile(3))):
            k_ref[side, i] = c

    get = lambda x, y: u_ref[x, y]
    (far_lo, near_lo), (near_hi, far_hi) = [[layer(rows, i, parts, ny, np_) for i in (0, 1)] for rows in messages]
    v_ref[1 : nx - 1] = v_in[1 : nx - 1]
    ends = {0: 0, nx - 1: 1}

    def put(x, y, total):
        if y == 0:
            dn_ends[ends[x]] = total
        elif y == ny - 1:
            up_ends[ends[x]] = total
        else:
            v_ref[x, y - 1] = total

    sweep(nx, ny, nz, range(ny), get, c_ref, near_lo, near_hi, None, put, None, (0, nx - 1))
    is_even = even("gy")
    for x in range(nx):
        dn, up = (dn_ends[ends[x]], up_ends[ends[x]]) if x in ends else (dn_in[x], up_in[x])
        one_ref[x] = jnp.where(is_even, up, dn)
        two_ref[x] = jnp.where(is_even, dn, up)

    def beyond(side, row, before, after, out_ref):
        def emit(y, total):
            out_ref[y] = total

        column(ny, nz, range(ny), row, before, after, lambda i, y: k_ref[side, i, pl.ds(y, 1), :], None, emit)

    beyond(0, near_lo, far_lo, lambda y: get(0, y), vlo_ref)
    beyond(1, near_hi, lambda y: get(nx - 1, y), far_hi, vhi_ref)


def close_kernel(
    nx, ny, np_, c_ref, rone_ref, rtwo_ref, one_ref, two_ref, low_ref, high_ref, xone_ref, xtwo_ref
):
    last = ny - 1
    below, above = sides(even("gy"), rone_ref, rtwo_ref)
    dn, up = sides(even("gy"), one_ref, two_ref)
    ends = {}
    for x in range(nx):
        rows = slice(x * np_, (x + 1) * np_)
        low = c_ref[YM, x, 0:1, :] * below(rows, slice(None))
        high = c_ref[YP, x, last : last + 1, :] * above(rows, slice(None))
        low_ref[x] = dn(x) + low
        high_ref[x] = up(x) + high
        ends[x] = low, high
    is_even = even("gx")
    for i in range(2):
        lo, hi = ends[0][i], ends[nx - 1][i]
        xone_ref[i] = jnp.where(is_even, hi, lo)
        xtwo_ref[i] = jnp.where(is_even, lo, hi)


def pieces(a):
    high = a.astype(BF16)
    rest = a - high.astype(F32)
    mid = rest.astype(BF16)
    return high, mid, (rest - mid.astype(F32)).astype(BF16)


def square(a):
    stack = jnp.concatenate(pieces(a), axis=0)
    return lax.dot_general(stack, stack, (((1,), (1,)), ((), ())), preferred_element_type=F32)


def fold(n, a):
    block = lambda i, j: a[i * n : i * n + n, j * n : j * n + n]
    return block(0, 0) + ((block(0, 1) + block(1, 0)) + (block(1, 1) + (block(0, 2) + block(2, 0))))


def border_kernel(
    nx, ny, np_, nz, one_ref, two_ref, v_ref, vlow_ref, vhigh_ref, c_ref, rone_ref, rtwo_ref, lo_ref, hi_ref,
    w_ref, wends_ref, wlow_ref, whigh_ref, g_ref,
):
    half = nx * np_
    get, _ = split(ny, vlow_ref, v_ref, vhigh_ref)

    received = sides(even("gy"), rone_ref, rtwo_ref)
    sent = sides(even("gy"), one_ref, two_ref)

    def ring(x, y):
        side, all_z = 0 if y == 0 else 1, slice(None)
        return received[side](pl.ds(half + x, 1), all_z) * sent[side](pl.ds(x * np_, np_), all_z)

    g_ref[...] = jnp.zeros_like(g_ref)

    def emit(x, y, total):
        if y == 0:
            wlow_ref[x] = total
        elif y == ny - 1:
            whigh_ref[x] = total
        else:
            w_ref[x, 0 if y == 1 else 1] = total
            g_ref[...] += square(total)

    ends = (0, 1, nx - 2, nx - 1)

    def emit_ends(x, y, total):
        wends_ref[ends.index(x), y - 2] = total
        g_ref[...] += square(total)

    lo, hi = face(lo_ref), face(hi_ref)
    sweep(nx, ny, nz, (0, 1, ny - 2, ny - 1), get, c_ref, lo, hi, ring, emit, (1, nx - 1), (0, nx - 1))
    sweep(nx, ny, nz, range(2, ny - 2), get, c_ref, lo, hi, None, emit_ends, None, ends)


def last_kernel(
    nx, ny, np_, copies, c_ref, rone_ref, rtwo_ref, xone_ref, xtwo_ref, ga_ref, gb_ref, wlow_in, whigh_in,
    wlow_ref, whigh_ref, g_ref,
):
    last = ny - 1
    gram = ga_ref[...] + gb_ref[...]
    below, above = sides(even("gy"), rone_ref, rtwo_ref)
    before, after = sides(even("gx"), xone_ref, xtwo_ref)
    for x in range(nx):
        low = wlow_in[x] + c_ref[YM, x, 0:1, :] * below(x)
        high = whigh_in[x] + c_ref[YP, x, last : last + 1, :] * above(x)
        if x == 0:
            low = low + c_ref[XM, x, 0:1, :] * before(0)
            high = high + c_ref[XM, x, last : last + 1, :] * before(1)
        if x == nx - 1:
            low = low + c_ref[XP, x, 0:1, :] * after(0)
            high = high + c_ref[XP, x, last : last + 1, :] * after(1)
        wlow_ref[x] = low
        whigh_ref[x] = high
        gram = gram + (square(low) + square(high))
    gram = fold(np_, gram)
    packed = jnp.concatenate([gram[8 * i : 8 * i + 8, :] for i in range(np_ // 8)], axis=1)
    for i in range(copies):
        g_ref[i] = packed


def factor_and_inverse(n, gram, factor_ref, inv_ref):
    eye = lax.broadcasted_iota(jnp.int32, (n, n), 0) == lax.broadcasted_iota(jnp.int32, (n, n), 1)
    a = jnp.concatenate([gram, jnp.where(eye, 1.0, 0.0)], axis=1)
    sub = lax.broadcasted_iota(jnp.int32, (n, 2 * n), 0)
    lane = lax.broadcasted_iota(jnp.int32, (1, n), 1)
    for k0 in range(0, n, BLOCK):
        cols = [jnp.broadcast_to(a[k0:, k : k + 1], (n - k0, 2 * n)) for k in range(k0, k0 + BLOCK)]
        low, rows = a[k0:], sub[k0:]
        for j in range(BLOCK):
            k = k0 + j
            r = lax.rsqrt(cols[j][j : j + 1, :])
            row = low[j : j + 1, :] * r
            factor_ref[k : k + 1, :] = jnp.where(lane >= k, row[:, :n], 0.0)
            inv_ref[k : k + 1, :] = row[:, n:]
            col = jnp.where(rows > k, cols[j] * r, 0.0)
            for m in range(j + 1, BLOCK):
                cols[m] = cols[m] - col * (cols[m][j : j + 1, :] * r)
            low = low - col * row
        a = low if k0 == 0 else jnp.concatenate([a[:k0], low], axis=0)


def basis_kernel(
    nx, ny, np_, scale, g_ref, w_ref, wside_ref, wends_ref, wlow_ref, whigh_ref, out_ref, factor_ref, inv_ref, stage, sems
):
    def get(x, y):
        if y in (0, ny - 1):
            return wlow_ref[x] if y == 0 else whigh_ref[x]
        if y in (1, ny - 2):
            return wside_ref[x, 0 if y == 1 else 1]
        ends = (0, 1, nx - 2, nx - 1)
        return wends_ref[ends.index(x), y - 2] if x in ends else w_ref[x - 2, y - 2]

    n = np_
    total = jnp.sum(g_ref[...], axis=0) * scale
    gram = jnp.concatenate([total[:, n * i : n * i + n] for i in range(n // 8)], axis=0)
    factor_and_inverse(n, gram, factor_ref, inv_ref)
    high, mid, low = pieces(inv_ref[...])
    none = jnp.zeros_like(high)
    left = jnp.concatenate(
        [jnp.concatenate(row, axis=1) for row in ((high, high, high), (mid, mid, none), (low, none, none))], axis=0
    )
    parts = wlow_ref.shape[2] // LANES
    group = parts * ny
    copies = []
    for x in range(nx):
        for y in range(ny):
            right = jnp.concatenate(pieces(get(x, y)), axis=0)
            terms = lax.dot_general(left, right, (((1,), (0,)), ((), ())), preferred_element_type=F32)
            block = terms[:n] + (terms[n : 2 * n] + terms[2 * n :])
            for h in range(parts):
                stage.at[x][pl.ds(h * ny + y, n, stride=group), :] = block[:, h * LANES : (h + 1) * LANES]
        copy = pltpu.make_async_copy(stage.at[x].reshape(n, group, LANES), out_ref.at[:, x], sems.at[x])
        copy.start()
        copies.append(copy)
    for copy in copies:
        copy.wait()


def on_device(probes, diffusion, velocity):
    np_, nx, ny, nz = probes.shape
    mx, my = lax.axis_size("gx"), lax.axis_size("gy")
    cells = mx * my * nx * ny * nz
    grid = (nx, ny, np_, nz)
    corner = (2, np_, nz)
    square_sum = (3 * np_, 3 * np_)
    plane = (nx, np_, nz)
    face_shape = (ny, np_, nz)
    tall = (nx * np_ + nx, nz)
    parts = nz // LANES
    tiled = lambda a: jnp.swapaxes(a.reshape(a.shape[:-1] + (parts, LANES)), -2, -3)
    tiles = tiled(probes)
    wide = ((2 * np_ + 4) * parts * ny, LANES)
    hbm = pl.BlockSpec(memory_space=pltpu.HBM)
    operands = [tiles, tiled(diffusion), tiled(velocity)]
    (one,), (two,) = [
        call(
            functools.partial(edge_kernel, nx, ny, np_, parts, upward),
            [tall],
            operands,
            scratch=[pltpu.VMEM((2, nx, nz), F32), pltpu.SemaphoreType.DMA],
            in_specs=[hbm] * 3,
            name=name,
        )
        for upward, name in ((True, "edge_one"), (False, "edge_two"))
    ]
    rone, rtwo = exchange(one, two, "gy")
    some = (nx, ny - 2, np_, nz)
    shapes = [some, plane, plane, face_shape, face_shape, (nx - 4, ny - 4, np_, nz), square_sum]

    def inside(tiles, diffusion, velocity):
        xone, xtwo = call(
            functools.partial(side_kernel, nx, ny, np_, parts),
            [wide, wide],
            [tiles, tiled(diffusion), tiled(velocity)],
            scratch=[pltpu.SemaphoreType.DMA],
            in_specs=[hbm] * 3,
            name="side",
        )
        xone, xtwo = exchange(xone, xtwo, "gx")
        u, coef, v, dn2, up2, w, gram = call(
            functools.partial(first_kernel, nx, ny, np_, nz),
            [grid, (7, nx, ny, nz), some, plane, plane, *shapes[5:]],
            [tiles.reshape(-1, LANES), diffusion, velocity],
            name="first",
        )
        made = call(
            functools.partial(outer_kernel, nx, ny, np_, nz),
            shapes[:5],
            [u, coef, xone, xtwo, v, dn2, up2],
            scratch=[pltpu.VMEM((2, 7, ny, nz), F32), pltpu.VMEM((2, np_, nz), F32), pltpu.VMEM((2, np_, nz), F32)],
            name="outer",
        )
        return (*made, w, gram)

    def outside(*_):
        return tuple(jnp.zeros(shape, F32) for shape in shapes)

    always = lax.axis_index("gx") >= 0
    v, one2, two2, vlo, vhi, w, gram = lax.cond(always, inside, outside, tiles, diffusion, velocity)
    rone2, rtwo2 = exchange(one2, two2, "gy")
    (coef,) = call(coefficient_kernel, [(7, nx, ny, nz)], [diffusion, velocity], name="coef")
    vlow, vhigh, xone3, xtwo3 = call(
        functools.partial(close_kernel, nx, ny, np_),
        [plane, plane, corner, corner],
        [coef, rone, rtwo, one2, two2],
        name="close",
    )
    xone3, xtwo3 = exchange(xone3, xtwo3, "gx")
    wside, wends, wlow, whigh, gram2 = call(
        functools.partial(border_kernel, nx, ny, np_, nz),
        [(nx, 2, np_, nz), (4, ny - 4, np_, nz), plane, plane, square_sum],
        [one, two, v, vlow, vhigh, coef, rone, rtwo, vlo, vhi],
        name="border",
    )
    wlow, whigh, grams = call(
        functools.partial(last_kernel, nx, ny, np_, mx * my),
        [plane, plane, (mx * my, 8, np_ * np_ // 8)],
        [coef, rone2, rtwo2, xone3, xtwo3, gram, gram2, wlow, whigh],
        name="last",
    )
    grams = lax.all_to_all(grams, ("gx", "gy"), 0, 0, tiled=True)
    basis, factor = call(
        functools.partial(basis_kernel, nx, ny, np_, 1.0 / cells),
        [(np_, nx, parts * ny, LANES), (np_, np_)],
        [grams, w, wside, wends, wlow, whigh],
        scratch=[
            pltpu.VMEM((np_, np_), F32),
            pltpu.VMEM((nx, np_ * parts * ny, LANES), F32),
            pltpu.SemaphoreType.DMA((nx,)),
        ],
        out_specs=[ANY, VMEM],
        name="basis",
    )
    basis = basis.reshape(np_, nx, parts, ny, LANES).transpose(0, 1, 3, 2, 4).reshape(np_, nx, ny, nz)
    return basis, factor


def solution(mesh):
    return jax.shard_map(
        on_device,
        mesh=mesh,
        in_specs=(P(None, "gx", "gy", None), P("gx", "gy", None), P(None, "gx", "gy", None)),
        out_specs=(P(None, "gx", "gy", None), P()),
        check_vma=False,
    )
```

```python
import functools

import jax
import jax.numpy as jnp
from jax import lax
from jax.experimental import pallas as pl
from jax.experimental.pallas import tpu as pltpu
from jax.sharding import PartitionSpec as P

F32 = jnp.float32
BF16 = jnp.bfloat16
VMEM = pl.BlockSpec(memory_space=pltpu.VMEM)
ANY = pl.BlockSpec(memory_space=pl.ANY)
LANES = 128
BLOCK = 32
W0, XP, XM, YP, YM, ZP, ZM = range(7)


def call(body, outs, ins, scratch=(), in_specs=None, out_specs=None, name=None, vmem=24, aliases=None):
    return pl.pallas_call(
        body,
        out_shape=[jax.ShapeDtypeStruct(s, F32) for s in outs],
        in_specs=in_specs or [VMEM] * len(ins),
        out_specs=out_specs or [VMEM] * len(outs),
        scratch_shapes=list(scratch),
        input_output_aliases=aliases or {},
        compiler_params=pltpu.CompilerParams(vmem_limit_bytes=vmem << 20),
        name=name,
    )(*ins)


def even(axis):
    return lax.rem(lax.axis_index(axis), 2) == 0


def swaps(count):
    pairs = [[(i, i + 1) for i in range(first, count - 1, 2)] for first in (0, 1)]
    return [[(i, j) for pair in each for i, j in (pair, pair[::-1])] for each in pairs]


def exchange(one, two, axis):
    first, second = swaps(lax.axis_size(axis))
    return lax.ppermute(one, axis, first), lax.ppermute(two, axis, second)


def sides(is_even, one, two):
    low = lambda *at: jnp.where(is_even, two[at], one[at])
    high = lambda *at: jnp.where(is_even, one[at], two[at])
    return low, high


def move(pairs, sem):
    copies = [pltpu.make_async_copy(src, dst, sem) for src, dst in pairs]
    for copy in copies:
        copy.start()
    for copy in copies:
        copy.wait()


def edge_kernel(nx, ny, np_, parts, upward, p_ref, d_ref, v_ref, out_ref, terms, sem):
    half = nx * np_

    def fill(y, sign):
        copies = []
        for h in range(parts):
            lanes = pl.ds(h * LANES, LANES)
            for x in range(nx):
                copies.append((p_ref.at[:, x, h, y, :], out_ref.at[pl.ds(x * np_, np_), lanes]))
            copies.append((d_ref.at[:, h, y, :], terms.at[0, :, lanes]))
            copies.append((v_ref.at[1, :, h, y, :], terms.at[1, :, lanes]))
        move(copies, sem)
        out_ref[half : half + nx, :] = terms[0] + sign * 0.5 * terms[1]

    is_up = even("gy") == upward

    @pl.when(is_up)
    def _():
        fill(ny - 1, -1.0)

    @pl.when(jnp.logical_not(is_up))
    def _():
        fill(0, 1.0)


def side_kernel(nx, ny, np_, parts, p_ref, d_ref, v_ref, one_ref, two_ref, sem):
    layers = np_ * 2 * parts * ny
    some = parts * ny

    def fill(hi_ref, lo_ref):
        copies = []
        for ref, first, outer in ((lo_ref, 0, 0), (hi_ref, nx - 2, nx - 1)):
            copies.append((p_ref.at[:, pl.ds(first, 2)], ref.at[pl.ds(0, layers)].reshape(np_, 2, parts, ny, LANES)))
            copies.append((d_ref.at[outer], ref.at[pl.ds(layers, some)].reshape(parts, ny, LANES)))
            copies.append((v_ref.at[:, outer], ref.at[pl.ds(layers + some, 3 * some)].reshape(3, parts, ny, LANES)))
        move(copies, sem)

    is_even = even("gx")

    @pl.when(is_even)
    def _():
        fill(one_ref, two_ref)

    @pl.when(jnp.logical_not(is_even))
    def _():
        fill(two_ref, one_ref)


def coefficients(d, vx, vy, vz):
    z = lax.broadcasted_iota(jnp.int32, d.shape, d.ndim - 1)
    return (
        1.0 - 6.0 * d,
        d - 0.5 * vx,
        d + 0.5 * vx,
        d - 0.5 * vy,
        d + 0.5 * vy,
        jnp.where(z == d.shape[-1] - 1, 0.0, d - 0.5 * vz),
        jnp.where(z == 0, 0.0, d + 0.5 * vz),
    )


def spread(nx, ny, np_, parts, p_ref, u_ref):
    for x in range(nx):
        for y in range(ny):
            for h in range(parts):
                block = p_ref[pl.ds((x * parts + h) * ny + y, np_, stride=nx * parts * ny), :]
                u_ref[x, y, :, h * LANES : (h + 1) * LANES] = block


def coefficient_kernel(d_ref, v_ref, c_ref):
    for i, c in enumerate(coefficients(d_ref[...], v_ref[0], v_ref[1], v_ref[2])):
        c_ref[i] = c


def column(ny, nz, ys, row, before, after, coef, ring, emit):
    rows = {y: row(y) for y in sorted({n for y in ys for n in (y - 1, y, y + 1) if 0 <= n < ny})}
    for y in ys:
        here = rows[y]
        k = lambda i: coef(i, y)
        total = k(W0) * here
        total = total + k(XP) * after(y) + k(XM) * before(y)
        if y + 1 < ny:
            total = total + k(YP) * rows[y + 1]
        elif ring is not None:
            total = total + k(YP) * ring(y)
        if y > 0:
            total = total + k(YM) * rows[y - 1]
        elif ring is not None:
            total = total + k(YM) * ring(y)
        total = total + k(ZP) * pltpu.roll(here, nz - 1, 1) + k(ZM) * pltpu.roll(here, 1, 1)
        emit(y, total)


def sweep(nx, ny, nz, ys, get, c_ref, lo, hi, ring, emit, loop=None, ends=None):
    def at(x, before, after):
        outside = None if ring is None else lambda y: ring(x, y)
        coef = lambda i, y: c_ref[i, x, pl.ds(y, 1), :]
        column(ny, nz, ys, lambda y: get(x, y), before, after, coef, outside, lambda y, total: emit(x, y, total))

    for x in ends:
        at(x, lo if x == 0 else lambda y: get(x - 1, y), hi if x == nx - 1 else lambda y: get(x + 1, y))
    if loop is not None:

        @pl.loop(*loop)
        def _(x):
            at(x, lambda y: get(x - 1, y), lambda y: get(x + 1, y))


def split(ny, low, inner, high):
    def get(x, y):
        return low[x] if y == 0 else high[x] if y == ny - 1 else inner[x, y - 1]

    def put(x, y, value):
        if y == 0:
            low[x] = value
        elif y == ny - 1:
            high[x] = value
        else:
            inner[x, y - 1] = value

    return get, put


def layer(rows, i, parts, ny, np_):
    def get(y):
        each = [rows(pl.ds((i * parts + h) * ny + y, np_, stride=2 * parts * ny), slice(None)) for h in range(parts)]
        return jnp.concatenate(each, axis=1)

    return get


def face(ref):
    return lambda y: ref[y]


def first_kernel(nx, ny, np_, nz, p_ref, d_ref, v_ref, u_ref, c_ref, out_ref, dn_ref, up_ref, w_ref, g_ref):
    spread(nx, ny, np_, nz // LANES, p_ref, u_ref)
    coefficient_kernel(d_ref, v_ref, c_ref)
    get, put = split(ny, dn_ref, out_ref, up_ref)
    sweep(nx, ny, nz, range(ny), lambda x, y: u_ref[x, y], c_ref, None, None, None, put, (1, nx - 1), ())
    g_ref[...] = jnp.zeros_like(g_ref)

    def emit(x, y, total):
        w_ref[x - 2, y - 2] = total
        g_ref[...] += square(total)

    sweep(nx, ny, nz, range(2, ny - 2), get, c_ref, None, None, None, emit, (2, nx - 2), ())


def outer_kernel(
    nx, ny, np_, nz, u_ref, c_ref, xone_ref, xtwo_ref, v_in, dn_in, up_in,
    v_ref, one_ref, two_ref, vlo_ref, vhi_ref, k_ref, dn_ends, up_ends,
):
    parts = nz // LANES
    layers = np_ * 2 * parts * ny
    messages = sides(even("gx"), xone_ref, xtwo_ref)
    for side, rows in enumerate(messages):
        tile = lambda i: jnp.concatenate(
            [rows(pl.ds(layers + (i * parts + h) * ny, ny), slice(None)) for h in range(parts)], axis=1
        )
        for i, c in enumerate(coefficients(tile(0), tile(1), tile(2), tile(3))):
            k_ref[side, i] = c

    get = lambda x, y: u_ref[x, y]
    (far_lo, near_lo), (near_hi, far_hi) = [[layer(rows, i, parts, ny, np_) for i in (0, 1)] for rows in messages]
    v_ref[1 : nx - 1] = v_in[1 : nx - 1]
    ends = {0: 0, nx - 1: 1}

    def put(x, y, total):
        if y == 0:
            dn_ends[ends[x]] = total
        elif y == ny - 1:
            up_ends[ends[x]] = total
        else:
            v_ref[x, y - 1] = total

    sweep(nx, ny, nz, range(ny), get, c_ref, near_lo, near_hi, None, put, None, (0, nx - 1))
    is_even = even("gy")
    for x in range(nx):
        dn, up = (dn_ends[ends[x]], up_ends[ends[x]]) if x in ends else (dn_in[x], up_in[x])
        one_ref[x] = jnp.where(is_even, up, dn)
        two_ref[x] = jnp.where(is_even, dn, up)

    def beyond(side, row, before, after, out_ref):
        def emit(y, total):
            out_ref[y] = total

        column(ny, nz, range(ny), row, before, after, lambda i, y: k_ref[side, i, pl.ds(y, 1), :], None, emit)

    beyond(0, near_lo, far_lo, lambda y: get(0, y), vlo_ref)
    beyond(1, near_hi, lambda y: get(nx - 1, y), far_hi, vhi_ref)


def close_kernel(
    nx, ny, np_, c_ref, rone_ref, rtwo_ref, one_ref, two_ref, low_ref, high_ref, xone_ref, xtwo_ref
):
    last = ny - 1
    below, above = sides(even("gy"), rone_ref, rtwo_ref)
    dn, up = sides(even("gy"), one_ref, two_ref)
    ends = {}
    for x in range(nx):
        rows = slice(x * np_, (x + 1) * np_)
        low = c_ref[YM, x, 0:1, :] * below(rows, slice(None))
        high = c_ref[YP, x, last : last + 1, :] * above(rows, slice(None))
        low_ref[x] = dn(x) + low
        high_ref[x] = up(x) + high
        ends[x] = low, high
    is_even = even("gx")
    for i in range(2):
        lo, hi = ends[0][i], ends[nx - 1][i]
        xone_ref[i] = jnp.where(is_even, hi, lo)
        xtwo_ref[i] = jnp.where(is_even, lo, hi)


def pieces(a):
    high = a.astype(BF16)
    rest = a - high.astype(F32)
    mid = rest.astype(BF16)
    return high, mid, (rest - mid.astype(F32)).astype(BF16)


def square(a):
    stack = jnp.concatenate(pieces(a), axis=0)
    return lax.dot_general(stack, stack, (((1,), (1,)), ((), ())), preferred_element_type=F32)


def fold(n, a):
    block = lambda i, j: a[i * n : i * n + n, j * n : j * n + n]
    return block(0, 0) + ((block(0, 1) + block(1, 0)) + (block(1, 1) + (block(0, 2) + block(2, 0))))


def border_kernel(
    nx, ny, np_, nz, one_ref, two_ref, v_ref, vlow_ref, vhigh_ref, c_ref, rone_ref, rtwo_ref, lo_ref, hi_ref,
    w_ref, wends_ref, wlow_ref, whigh_ref, g_ref,
):
    half = nx * np_
    get, _ = split(ny, vlow_ref, v_ref, vhigh_ref)

    received = sides(even("gy"), rone_ref, rtwo_ref)
    sent = sides(even("gy"), one_ref, two_ref)

    def ring(x, y):
        side, all_z = 0 if y == 0 else 1, slice(None)
        return received[side](pl.ds(half + x, 1), all_z) * sent[side](pl.ds(x * np_, np_), all_z)

    g_ref[...] = jnp.zeros_like(g_ref)

    def emit(x, y, total):
        if y == 0:
            wlow_ref[x] = total
        elif y == ny - 1:
            whigh_ref[x] = total
        else:
            w_ref[x, 0 if y == 1 else 1] = total
            g_ref[...] += square(total)

    ends = (0, 1, nx - 2, nx - 1)

    def emit_ends(x, y, total):
        wends_ref[ends.index(x), y - 2] = total
        g_ref[...] += square(total)

    lo, hi = face(lo_ref), face(hi_ref)
    sweep(nx, ny, nz, (0, 1, ny - 2, ny - 1), get, c_ref, lo, hi, ring, emit, (1, nx - 1), (0, nx - 1))
    sweep(nx, ny, nz, range(2, ny - 2), get, c_ref, lo, hi, None, emit_ends, None, ends)


def last_kernel(
    nx, ny, np_, copies, c_ref, rone_ref, rtwo_ref, xone_ref, xtwo_ref, ga_ref, gb_ref, wlow_in, whigh_in,
    wlow_ref, whigh_ref, g_ref,
):
    last = ny - 1
    gram = ga_ref[...] + gb_ref[...]
    below, above = sides(even("gy"), rone_ref, rtwo_ref)
    before, after = sides(even("gx"), xone_ref, xtwo_ref)
    for x in range(nx):
        low = wlow_in[x] + c_ref[YM, x, 0:1, :] * below(x)
        high = whigh_in[x] + c_ref[YP, x, last : last + 1, :] * above(x)
        if x == 0:
            low = low + c_ref[XM, x, 0:1, :] * before(0)
            high = high + c_ref[XM, x, last : last + 1, :] * before(1)
        if x == nx - 1:
            low = low + c_ref[XP, x, 0:1, :] * after(0)
            high = high + c_ref[XP, x, last : last + 1, :] * after(1)
        wlow_ref[x] = low
        whigh_ref[x] = high
        gram = gram + (square(low) + square(high))
    gram = fold(np_, gram)
    packed = jnp.concatenate([gram[8 * i : 8 * i + 8, :] for i in range(np_ // 8)], axis=1)
    for i in range(copies):
        g_ref[i] = packed


def factor_and_inverse(n, gram, factor_ref, inv_ref):
    eye = lax.broadcasted_iota(jnp.int32, (n, n), 0) == lax.broadcasted_iota(jnp.int32, (n, n), 1)
    a = jnp.concatenate([gram, jnp.where(eye, 1.0, 0.0)], axis=1)
    sub = lax.broadcasted_iota(jnp.int32, (n, 2 * n), 0)
    lane = lax.broadcasted_iota(jnp.int32, (1, n), 1)
    for k0 in range(0, n, BLOCK):
        cols = [jnp.broadcast_to(a[k0:, k : k + 1], (n - k0, 2 * n)) for k in range(k0, k0 + BLOCK)]
        low, rows = a[k0:], sub[k0:]
        for j in range(BLOCK):
            k = k0 + j
            r = lax.rsqrt(cols[j][j : j + 1, :])
            row = low[j : j + 1, :] * r
            factor_ref[k : k + 1, :] = jnp.where(lane >= k, row[:, :n], 0.0)
            inv_ref[k : k + 1, :] = row[:, n:]
            col = jnp.where(rows > k, cols[j] * r, 0.0)
            for m in range(j + 1, BLOCK):
                cols[m] = cols[m] - col * (cols[m][j : j + 1, :] * r)
            low = low - col * row
        a = low if k0 == 0 else jnp.concatenate([a[:k0], low], axis=0)


def basis_kernel(
    nx, ny, np_, scale, g_ref, w_ref, wside_ref, wends_ref, wlow_ref, whigh_ref, out_ref, factor_ref, inv_ref, stage, sems
):
    def get(x, y):
        if y in (0, ny - 1):
            return wlow_ref[x] if y == 0 else whigh_ref[x]
        if y in (1, ny - 2):
            return wside_ref[x, 0 if y == 1 else 1]
        ends = (0, 1, nx - 2, nx - 1)
        return wends_ref[ends.index(x), y - 2] if x in ends else w_ref[x - 2, y - 2]

    n = np_
    total = jnp.sum(g_ref[...], axis=0) * scale
    gram = jnp.concatenate([total[:, n * i : n * i + n] for i in range(n // 8)], axis=0)
    factor_and_inverse(n, gram, factor_ref, inv_ref)
    high, mid, low = pieces(inv_ref[...])
    none = jnp.zeros_like(high)
    left = jnp.concatenate(
        [jnp.concatenate(row, axis=1) for row in ((high, high, high), (mid, mid, none), (low, none, none))], axis=0
    )
    parts = wlow_ref.shape[2] // LANES
    group = parts * ny
    copies = []
    for x in range(nx):
        for y in range(ny):
            right = jnp.concatenate(pieces(get(x, y)), axis=0)
            terms = lax.dot_general(left, right, (((1,), (0,)), ((), ())), preferred_element_type=F32)
            block = terms[:n] + (terms[n : 2 * n] + terms[2 * n :])
            for h in range(parts):
                stage.at[x][pl.ds(h * ny + y, n, stride=group), :] = block[:, h * LANES : (h + 1) * LANES]
        copy = pltpu.make_async_copy(stage.at[x].reshape(n, group, LANES), out_ref.at[:, x], sems.at[x])
        copy.start()
        copies.append(copy)
    for copy in copies:
        copy.wait()


def on_device(probes, diffusion, velocity):
    np_, nx, ny, nz = probes.shape
    mx, my = lax.axis_size("gx"), lax.axis_size("gy")
    cells = mx * my * nx * ny * nz
    grid = (nx, ny, np_, nz)
    corner = (2, np_, nz)
    square_sum = (3 * np_, 3 * np_)
    plane = (nx, np_, nz)
    face_shape = (ny, np_, nz)
    tall = (nx * np_ + nx, nz)
    parts = nz // LANES
    tiled = lambda a: jnp.swapaxes(a.reshape(a.shape[:-1] + (parts, LANES)), -2, -3)
    tiles = tiled(probes)
    wide = ((2 * np_ + 4) * parts * ny, LANES)
    hbm = pl.BlockSpec(memory_space=pltpu.HBM)
    operands = [tiles, tiled(diffusion), tiled(velocity)]
    (one,), (two,) = [
        call(
            functools.partial(edge_kernel, nx, ny, np_, parts, upward),
            [tall],
            operands,
            scratch=[pltpu.VMEM((2, nx, nz), F32), pltpu.SemaphoreType.DMA],
            in_specs=[hbm] * 3,
            name=name,
        )
        for upward, name in ((True, "edge_one"), (False, "edge_two"))
    ]
    rone, rtwo = exchange(one, two, "gy")
    some = (nx, ny - 2, np_, nz)
    shapes = [some, plane, plane, face_shape, face_shape, (nx - 4, ny - 4, np_, nz), square_sum]

    def inside(tiles, diffusion, velocity):
        xone, xtwo = call(
            functools.partial(side_kernel, nx, ny, np_, parts),
            [wide, wide],
            [tiles, tiled(diffusion), tiled(velocity)],
            scratch=[pltpu.SemaphoreType.DMA],
            in_specs=[hbm] * 3,
            name="side",
        )
        xone, xtwo = exchange(xone, xtwo, "gx")
        u, coef, v, dn2, up2, w, gram = call(
            functools.partial(first_kernel, nx, ny, np_, nz),
            [grid, (7, nx, ny, nz), some, plane, plane, *shapes[5:]],
            [tiles.reshape(-1, LANES), diffusion, velocity],
            name="first",
        )
        made = call(
            functools.partial(outer_kernel, nx, ny, np_, nz),
            shapes[:5],
            [u, coef, xone, xtwo, v, dn2, up2],
            scratch=[pltpu.VMEM((2, 7, ny, nz), F32), pltpu.VMEM((2, np_, nz), F32), pltpu.VMEM((2, np_, nz), F32)],
            name="outer",
        )
        return (*made, w, gram)

    def outside(*_):
        return tuple(jnp.zeros(shape, F32) for shape in shapes)

    always = lax.axis_index("gx") >= 0
    v, one2, two2, vlo, vhi, w, gram = lax.cond(always, inside, outside, tiles, diffusion, velocity)
    rone2, rtwo2 = exchange(one2, two2, "gy")
    (coef,) = call(coefficient_kernel, [(7, nx, ny, nz)], [diffusion, velocity], name="coef")
    vlow, vhigh, xone3, xtwo3 = call(
        functools.partial(close_kernel, nx, ny, np_),
        [plane, plane, corner, corner],
        [coef, rone, rtwo, one2, two2],
        name="close",
    )
    xone3, xtwo3 = exchange(xone3, xtwo3, "gx")
    wside, wends, wlow, whigh, gram2 = call(
        functools.partial(border_kernel, nx, ny, np_, nz),
        [(nx, 2, np_, nz), (4, ny - 4, np_, nz), plane, plane, square_sum],
        [one, two, v, vlow, vhigh, coef, rone, rtwo, vlo, vhi],
        name="border",
    )
    wlow, whigh, grams = call(
        functools.partial(last_kernel, nx, ny, np_, mx * my),
        [plane, plane, (mx * my, 8, np_ * np_ // 8)],
        [coef, rone2, rtwo2, xone3, xtwo3, gram, gram2, wlow, whigh],
        name="last",
    )
    grams = lax.all_to_all(grams, ("gx", "gy"), 0, 0, tiled=True)
    basis, factor = call(
        functools.partial(basis_kernel, nx, ny, np_, 1.0 / cells),
        [(np_, nx, parts * ny, LANES), (np_, np_)],
        [grams, w, wside, wends, wlow, whigh],
        scratch=[
            pltpu.VMEM((np_, np_), F32),
            pltpu.VMEM((nx, np_ * parts * ny, LANES), F32),
            pltpu.SemaphoreType.DMA((nx,)),
        ],
        out_specs=[ANY, VMEM],
        name="basis",
    )
    basis = basis.reshape(np_, nx, parts, ny, LANES).transpose(0, 1, 3, 2, 4).reshape(np_, nx, ny, nz)
    return basis, factor


def solution(mesh):
    return jax.shard_map(
        on_device,
        mesh=mesh,
        in_specs=(P(None, "gx", "gy", None), P("gx", "gy", None), P(None, "gx", "gy", None)),
        out_specs=(P(None, "gx", "gy", None), P()),
        check_vma=False,
    )
```

```python
import functools

import jax
import jax.numpy as jnp
from jax import lax
from jax.experimental import pallas as pl
from jax.experimental.pallas import tpu as pltpu
from jax.sharding import PartitionSpec as P

F32 = jnp.float32
BF16 = jnp.bfloat16
VMEM = pl.BlockSpec(memory_space=pltpu.VMEM)
ANY = pl.BlockSpec(memory_space=pl.ANY)
LANES = 128
BLOCK = 16
W0, XP, XM, YP, YM, ZP, ZM = range(7)


def call(body, outs, ins, scratch=(), in_specs=None, out_specs=None, name=None, vmem=24, aliases=None):
    return pl.pallas_call(
        body,
        out_shape=[jax.ShapeDtypeStruct(s, F32) for s in outs],
        in_specs=in_specs or [VMEM] * len(ins),
        out_specs=out_specs or [VMEM] * len(outs),
        scratch_shapes=list(scratch),
        input_output_aliases=aliases or {},
        compiler_params=pltpu.CompilerParams(vmem_limit_bytes=vmem << 20),
        name=name,
    )(*ins)


def even(axis):
    return lax.rem(lax.axis_index(axis), 2) == 0


def swaps(count):
    pairs = [[(i, i + 1) for i in range(first, count - 1, 2)] for first in (0, 1)]
    return [[(i, j) for pair in each for i, j in (pair, pair[::-1])] for each in pairs]


def exchange(one, two, axis):
    first, second = swaps(lax.axis_size(axis))
    return lax.ppermute(one, axis, first), lax.ppermute(two, axis, second)


def sides(is_even, one, two):
    low = lambda *at: jnp.where(is_even, two[at], one[at])
    high = lambda *at: jnp.where(is_even, one[at], two[at])
    return low, high


def move(pairs, sem):
    copies = [pltpu.make_async_copy(src, dst, sem) for src, dst in pairs]
    for copy in copies:
        copy.start()
    for copy in copies:
        copy.wait()


def edge_kernel(nx, ny, np_, parts, upward, p_ref, d_ref, v_ref, out_ref, terms, sem):
    half = nx * np_

    def fill(y, sign):
        copies = []
        for h in range(parts):
            lanes = pl.ds(h * LANES, LANES)
            for x in range(nx):
                copies.append((p_ref.at[:, x, h, y, :], out_ref.at[pl.ds(x * np_, np_), lanes]))
            copies.append((d_ref.at[:, h, y, :], terms.at[0, :, lanes]))
            copies.append((v_ref.at[1, :, h, y, :], terms.at[1, :, lanes]))
        move(copies, sem)
        out_ref[half : half + nx, :] = terms[0] + sign * 0.5 * terms[1]

    is_up = even("gy") == upward

    @pl.when(is_up)
    def _():
        fill(ny - 1, -1.0)

    @pl.when(jnp.logical_not(is_up))
    def _():
        fill(0, 1.0)


def side_kernel(nx, ny, np_, parts, p_ref, d_ref, v_ref, one_ref, two_ref, sem):
    layers = np_ * 2 * parts * ny
    some = parts * ny

    def fill(hi_ref, lo_ref):
        copies = []
        for ref, first, outer in ((lo_ref, 0, 0), (hi_ref, nx - 2, nx - 1)):
            copies.append((p_ref.at[:, pl.ds(first, 2)], ref.at[pl.ds(0, layers)].reshape(np_, 2, parts, ny, LANES)))
            copies.append((d_ref.at[outer], ref.at[pl.ds(layers, some)].reshape(parts, ny, LANES)))
            copies.append((v_ref.at[:, outer], ref.at[pl.ds(layers + some, 3 * some)].reshape(3, parts, ny, LANES)))
        move(copies, sem)

    is_even = even("gx")

    @pl.when(is_even)
    def _():
        fill(one_ref, two_ref)

    @pl.when(jnp.logical_not(is_even))
    def _():
        fill(two_ref, one_ref)


def coefficients(d, vx, vy, vz):
    z = lax.broadcasted_iota(jnp.int32, d.shape, d.ndim - 1)
    return (
        1.0 - 6.0 * d,
        d - 0.5 * vx,
        d + 0.5 * vx,
        d - 0.5 * vy,
        d + 0.5 * vy,
        jnp.where(z == d.shape[-1] - 1, 0.0, d - 0.5 * vz),
        jnp.where(z == 0, 0.0, d + 0.5 * vz),
    )


def spread(nx, ny, np_, parts, p_ref, u_ref):
    for x in range(nx):
        for y in range(ny):
            for h in range(parts):
                block = p_ref[pl.ds((x * parts + h) * ny + y, np_, stride=nx * parts * ny), :]
                u_ref[x, y, :, h * LANES : (h + 1) * LANES] = block


def coefficient_kernel(d_ref, v_ref, c_ref):
    for i, c in enumerate(coefficients(d_ref[...], v_ref[0], v_ref[1], v_ref[2])):
        c_ref[i] = c


def column(ny, nz, ys, row, before, after, coef, ring, emit):
    rows = {y: row(y) for y in sorted({n for y in ys for n in (y - 1, y, y + 1) if 0 <= n < ny})}
    for y in ys:
        here = rows[y]
        k = lambda i: coef(i, y)
        total = k(W0) * here
        total = total + k(XP) * after(y) + k(XM) * before(y)
        if y + 1 < ny:
            total = total + k(YP) * rows[y + 1]
        elif ring is not None:
            total = total + k(YP) * ring(y)
        if y > 0:
            total = total + k(YM) * rows[y - 1]
        elif ring is not None:
            total = total + k(YM) * ring(y)
        total = total + k(ZP) * pltpu.roll(here, nz - 1, 1) + k(ZM) * pltpu.roll(here, 1, 1)
        emit(y, total)


def sweep(nx, ny, nz, ys, get, c_ref, lo, hi, ring, emit, loop=None, ends=None):
    def at(x, before, after):
        outside = None if ring is None else lambda y: ring(x, y)
        coef = lambda i, y: c_ref[i, x, pl.ds(y, 1), :]
        column(ny, nz, ys, lambda y: get(x, y), before, after, coef, outside, lambda y, total: emit(x, y, total))

    for x in ends:
        at(x, lo if x == 0 else lambda y: get(x - 1, y), hi if x == nx - 1 else lambda y: get(x + 1, y))
    if loop is not None:

        @pl.loop(*loop)
        def _(x):
            at(x, lambda y: get(x - 1, y), lambda y: get(x + 1, y))


def split(ny, low, inner, high):
    def get(x, y):
        return low[x] if y == 0 else high[x] if y == ny - 1 else inner[x, y - 1]

    def put(x, y, value):
        if y == 0:
            low[x] = value
        elif y == ny - 1:
            high[x] = value
        else:
            inner[x, y - 1] = value

    return get, put


def layer(rows, i, parts, ny, np_):
    def get(y):
        each = [rows(pl.ds((i * parts + h) * ny + y, np_, stride=2 * parts * ny), slice(None)) for h in range(parts)]
        return jnp.concatenate(each, axis=1)

    return get


def face(ref):
    return lambda y: ref[y]


def first_kernel(nx, ny, np_, nz, p_ref, d_ref, v_ref, u_ref, c_ref, out_ref, dn_ref, up_ref, w_ref, g_ref):
    spread(nx, ny, np_, nz // LANES, p_ref, u_ref)
    coefficient_kernel(d_ref, v_ref, c_ref)
    get, put = split(ny, dn_ref, out_ref, up_ref)
    sweep(nx, ny, nz, range(ny), lambda x, y: u_ref[x, y], c_ref, None, None, None, put, (1, nx - 1), ())
    g_ref[...] = jnp.zeros_like(g_ref)

    def emit(x, y, total):
        w_ref[x - 2, y - 2] = total
        g_ref[...] += square(total)

    sweep(nx, ny, nz, range(2, ny - 2), get, c_ref, None, None, None, emit, (2, nx - 2), ())


def outer_kernel(
    nx, ny, np_, nz, u_ref, c_ref, xone_ref, xtwo_ref, v_in, dn_in, up_in,
    v_ref, one_ref, two_ref, vlo_ref, vhi_ref, k_ref, dn_ends, up_ends,
):
    parts = nz // LANES
    layers = np_ * 2 * parts * ny
    messages = sides(even("gx"), xone_ref, xtwo_ref)
    for side, rows in enumerate(messages):
        tile = lambda i: jnp.concatenate(
            [rows(pl.ds(layers + (i * parts + h) * ny, ny), slice(None)) for h in range(parts)], axis=1
        )
        for i, c in enumerate(coefficients(tile(0), tile(1), tile(2), tile(3))):
            k_ref[side, i] = c

    get = lambda x, y: u_ref[x, y]
    (far_lo, near_lo), (near_hi, far_hi) = [[layer(rows, i, parts, ny, np_) for i in (0, 1)] for rows in messages]
    v_ref[1 : nx - 1] = v_in[1 : nx - 1]
    ends = {0: 0, nx - 1: 1}

    def put(x, y, total):
        if y == 0:
            dn_ends[ends[x]] = total
        elif y == ny - 1:
            up_ends[ends[x]] = total
        else:
            v_ref[x, y - 1] = total

    sweep(nx, ny, nz, range(ny), get, c_ref, near_lo, near_hi, None, put, None, (0, nx - 1))
    is_even = even("gy")
    for x in range(nx):
        dn, up = (dn_ends[ends[x]], up_ends[ends[x]]) if x in ends else (dn_in[x], up_in[x])
        one_ref[x] = jnp.where(is_even, up, dn)
        two_ref[x] = jnp.where(is_even, dn, up)

    def beyond(side, row, before, after, out_ref):
        def emit(y, total):
            out_ref[y] = total

        column(ny, nz, range(ny), row, before, after, lambda i, y: k_ref[side, i, pl.ds(y, 1), :], None, emit)

    beyond(0, near_lo, far_lo, lambda y: get(0, y), vlo_ref)
    beyond(1, near_hi, lambda y: get(nx - 1, y), far_hi, vhi_ref)


def close_kernel(
    nx, ny, np_, c_ref, rone_ref, rtwo_ref, one_ref, two_ref, low_ref, high_ref, xone_ref, xtwo_ref
):
    last = ny - 1
    below, above = sides(even("gy"), rone_ref, rtwo_ref)
    dn, up = sides(even("gy"), one_ref, two_ref)
    ends = {}
    for x in range(nx):
        rows = slice(x * np_, (x + 1) * np_)
        low = c_ref[YM, x, 0:1, :] * below(rows, slice(None))
        high = c_ref[YP, x, last : last + 1, :] * above(rows, slice(None))
        low_ref[x] = dn(x) + low
        high_ref[x] = up(x) + high
        ends[x] = low, high
    is_even = even("gx")
    for i in range(2):
        lo, hi = ends[0][i], ends[nx - 1][i]
        xone_ref[i] = jnp.where(is_even, hi, lo)
        xtwo_ref[i] = jnp.where(is_even, lo, hi)


def pieces(a):
    high = a.astype(BF16)
    rest = a - high.astype(F32)
    mid = rest.astype(BF16)
    return high, mid, (rest - mid.astype(F32)).astype(BF16)


def square(a):
    stack = jnp.concatenate(pieces(a), axis=0)
    return lax.dot_general(stack, stack, (((1,), (1,)), ((), ())), preferred_element_type=F32)


def fold(n, a):
    block = lambda i, j: a[i * n : i * n + n, j * n : j * n + n]
    return block(0, 0) + ((block(0, 1) + block(1, 0)) + (block(1, 1) + (block(0, 2) + block(2, 0))))


def border_kernel(
    nx, ny, np_, nz, one_ref, two_ref, v_ref, vlow_ref, vhigh_ref, c_ref, rone_ref, rtwo_ref, lo_ref, hi_ref,
    w_ref, wends_ref, wlow_ref, whigh_ref, g_ref,
):
    half = nx * np_
    get, _ = split(ny, vlow_ref, v_ref, vhigh_ref)

    received = sides(even("gy"), rone_ref, rtwo_ref)
    sent = sides(even("gy"), one_ref, two_ref)

    def ring(x, y):
        side, all_z = 0 if y == 0 else 1, slice(None)
        return received[side](pl.ds(half + x, 1), all_z) * sent[side](pl.ds(x * np_, np_), all_z)

    g_ref[...] = jnp.zeros_like(g_ref)

    def emit(x, y, total):
        if y == 0:
            wlow_ref[x] = total
        elif y == ny - 1:
            whigh_ref[x] = total
        else:
            w_ref[x, 0 if y == 1 else 1] = total
            g_ref[...] += square(total)

    ends = (0, 1, nx - 2, nx - 1)

    def emit_ends(x, y, total):
        wends_ref[ends.index(x), y - 2] = total
        g_ref[...] += square(total)

    lo, hi = face(lo_ref), face(hi_ref)
    sweep(nx, ny, nz, (0, 1, ny - 2, ny - 1), get, c_ref, lo, hi, ring, emit, (1, nx - 1), (0, nx - 1))
    sweep(nx, ny, nz, range(2, ny - 2), get, c_ref, lo, hi, None, emit_ends, None, ends)


def last_kernel(
    nx, ny, np_, copies, c_ref, rone_ref, rtwo_ref, xone_ref, xtwo_ref, ga_ref, gb_ref, wlow_in, whigh_in,
    wlow_ref, whigh_ref, g_ref,
):
    last = ny - 1
    gram = ga_ref[...] + gb_ref[...]
    below, above = sides(even("gy"), rone_ref, rtwo_ref)
    before, after = sides(even("gx"), xone_ref, xtwo_ref)
    for x in range(nx):
        low = wlow_in[x] + c_ref[YM, x, 0:1, :] * below(x)
        high = whigh_in[x] + c_ref[YP, x, last : last + 1, :] * above(x)
        if x == 0:
            low = low + c_ref[XM, x, 0:1, :] * before(0)
            high = high + c_ref[XM, x, last : last + 1, :] * before(1)
        if x == nx - 1:
            low = low + c_ref[XP, x, 0:1, :] * after(0)
            high = high + c_ref[XP, x, last : last + 1, :] * after(1)
        wlow_ref[x] = low
        whigh_ref[x] = high
        gram = gram + (square(low) + square(high))
    gram = fold(np_, gram)
    packed = jnp.concatenate([gram[8 * i : 8 * i + 8, :] for i in range(np_ // 8)], axis=1)
    for i in range(copies):
        g_ref[i] = packed


def factor_and_inverse(n, gram, factor_ref, inv_ref):
    eye = lax.broadcasted_iota(jnp.int32, (n, n), 0) == lax.broadcasted_iota(jnp.int32, (n, n), 1)
    a = jnp.concatenate([gram, jnp.where(eye, 1.0, 0.0)], axis=1)
    sub = lax.broadcasted_iota(jnp.int32, (n, 2 * n), 0)
    lane = lax.broadcasted_iota(jnp.int32, (1, n), 1)
    for k0 in range(0, n, BLOCK):
        cols = [jnp.broadcast_to(a[k0:, k : k + 1], (n - k0, 2 * n)) for k in range(k0, k0 + BLOCK)]
        low, rows = a[k0:], sub[k0:]
        for j in range(BLOCK):
            k = k0 + j
            r = lax.rsqrt(cols[j][j : j + 1, :])
            row = low[j : j + 1, :] * r
            factor_ref[k : k + 1, :] = jnp.where(lane >= k, row[:, :n], 0.0)
            inv_ref[k : k + 1, :] = row[:, n:]
            col = jnp.where(rows > k, cols[j] * r, 0.0)
            for m in range(j + 1, BLOCK):
                cols[m] = cols[m] - col * (cols[m][j : j + 1, :] * r)
            low = low - col * row
        a = low if k0 == 0 else jnp.concatenate([a[:k0], low], axis=0)


def basis_kernel(
    nx, ny, np_, scale, g_ref, w_ref, wside_ref, wends_ref, wlow_ref, whigh_ref, out_ref, factor_ref, inv_ref, stage, sems
):
    def get(x, y):
        if y in (0, ny - 1):
            return wlow_ref[x] if y == 0 else whigh_ref[x]
        if y in (1, ny - 2):
            return wside_ref[x, 0 if y == 1 else 1]
        ends = (0, 1, nx - 2, nx - 1)
        return wends_ref[ends.index(x), y - 2] if x in ends else w_ref[x - 2, y - 2]

    n = np_
    total = jnp.sum(g_ref[...], axis=0) * scale
    gram = jnp.concatenate([total[:, n * i : n * i + n] for i in range(n // 8)], axis=0)
    factor_and_inverse(n, gram, factor_ref, inv_ref)
    high, mid, low = pieces(inv_ref[...])
    none = jnp.zeros_like(high)
    left = jnp.concatenate(
        [jnp.concatenate(row, axis=1) for row in ((high, high, high), (mid, mid, none), (low, none, none))], axis=0
    )
    parts = wlow_ref.shape[2] // LANES
    group = parts * ny
    copies = []
    for x in range(nx):
        for y in range(ny):
            right = jnp.concatenate(pieces(get(x, y)), axis=0)
            terms = lax.dot_general(left, right, (((1,), (0,)), ((), ())), preferred_element_type=F32)
            block = terms[:n] + (terms[n : 2 * n] + terms[2 * n :])
            for h in range(parts):
                stage.at[x][pl.ds(h * ny + y, n, stride=group), :] = block[:, h * LANES : (h + 1) * LANES]
        slab = stage.at[x].reshape(n, group, LANES)
        for p in range(0, n, 8):
            copy = pltpu.make_async_copy(slab.at[pl.ds(p, 8)], out_ref.at[pl.ds(p, 8), x], sems.at[x])
            copy.start()
            copies.append(copy)
    for copy in copies:
        copy.wait()


def on_device(probes, diffusion, velocity):
    np_, nx, ny, nz = probes.shape
    mx, my = lax.axis_size("gx"), lax.axis_size("gy")
    cells = mx * my * nx * ny * nz
    grid = (nx, ny, np_, nz)
    corner = (2, np_, nz)
    square_sum = (3 * np_, 3 * np_)
    plane = (nx, np_, nz)
    face_shape = (ny, np_, nz)
    tall = (nx * np_ + nx, nz)
    parts = nz // LANES
    tiled = lambda a: jnp.swapaxes(a.reshape(a.shape[:-1] + (parts, LANES)), -2, -3)
    tiles = tiled(probes)
    wide = ((2 * np_ + 4) * parts * ny, LANES)
    hbm = pl.BlockSpec(memory_space=pltpu.HBM)
    operands = [tiles, tiled(diffusion), tiled(velocity)]
    (one,), (two,) = [
        call(
            functools.partial(edge_kernel, nx, ny, np_, parts, upward),
            [tall],
            operands,
            scratch=[pltpu.VMEM((2, nx, nz), F32), pltpu.SemaphoreType.DMA],
            in_specs=[hbm] * 3,
            name=name,
        )
        for upward, name in ((True, "edge_one"), (False, "edge_two"))
    ]
    rone, rtwo = exchange(one, two, "gy")
    some = (nx, ny - 2, np_, nz)
    shapes = [some, plane, plane, face_shape, face_shape, (nx - 4, ny - 4, np_, nz), square_sum]

    def inside(tiles, diffusion, velocity):
        xone, xtwo = call(
            functools.partial(side_kernel, nx, ny, np_, parts),
            [wide, wide],
            [tiles, tiled(diffusion), tiled(velocity)],
            scratch=[pltpu.SemaphoreType.DMA],
            in_specs=[hbm] * 3,
            name="side",
        )
        xone, xtwo = exchange(xone, xtwo, "gx")
        u, coef, v, dn2, up2, w, gram = call(
            functools.partial(first_kernel, nx, ny, np_, nz),
            [grid, (7, nx, ny, nz), some, plane, plane, *shapes[5:]],
            [tiles.reshape(-1, LANES), diffusion, velocity],
            name="first",
        )
        made = call(
            functools.partial(outer_kernel, nx, ny, np_, nz),
            shapes[:5],
            [u, coef, xone, xtwo, v, dn2, up2],
            scratch=[pltpu.VMEM((2, 7, ny, nz), F32), pltpu.VMEM((2, np_, nz), F32), pltpu.VMEM((2, np_, nz), F32)],
            name="outer",
        )
        return (*made, w, gram)

    def outside(*_):
        return tuple(jnp.zeros(shape, F32) for shape in shapes)

    always = lax.axis_index("gx") >= 0
    v, one2, two2, vlo, vhi, w, gram = lax.cond(always, inside, outside, tiles, diffusion, velocity)
    rone2, rtwo2 = exchange(one2, two2, "gy")
    (coef,) = call(coefficient_kernel, [(7, nx, ny, nz)], [diffusion, velocity], name="coef")
    vlow, vhigh, xone3, xtwo3 = call(
        functools.partial(close_kernel, nx, ny, np_),
        [plane, plane, corner, corner],
        [coef, rone, rtwo, one2, two2],
        name="close",
    )
    xone3, xtwo3 = exchange(xone3, xtwo3, "gx")
    wside, wends, wlow, whigh, gram2 = call(
        functools.partial(border_kernel, nx, ny, np_, nz),
        [(nx, 2, np_, nz), (4, ny - 4, np_, nz), plane, plane, square_sum],
        [one, two, v, vlow, vhigh, coef, rone, rtwo, vlo, vhi],
        name="border",
    )
    wlow, whigh, grams = call(
        functools.partial(last_kernel, nx, ny, np_, mx * my),
        [plane, plane, (mx * my, 8, np_ * np_ // 8)],
        [coef, rone2, rtwo2, xone3, xtwo3, gram, gram2, wlow, whigh],
        name="last",
    )
    grams = lax.all_to_all(grams, ("gx", "gy"), 0, 0, tiled=True)
    basis, factor = call(
        functools.partial(basis_kernel, nx, ny, np_, 1.0 / cells),
        [(np_, nx, parts * ny, LANES), (np_, np_)],
        [grams, w, wside, wends, wlow, whigh],
        scratch=[
            pltpu.VMEM((np_, np_), F32),
            pltpu.VMEM((nx, np_ * parts * ny, LANES), F32),
            pltpu.SemaphoreType.DMA((nx,)),
        ],
        out_specs=[ANY, VMEM],
        name="basis",
    )
    basis = basis.reshape(np_, nx, parts, ny, LANES).transpose(0, 1, 3, 2, 4).reshape(np_, nx, ny, nz)
    return basis, factor


def solution(mesh):
    return jax.shard_map(
        on_device,
        mesh=mesh,
        in_specs=(P(None, "gx", "gy", None), P("gx", "gy", None), P(None, "gx", "gy", None)),
        out_specs=(P(None, "gx", "gy", None), P()),
        check_vma=False,
    )
```
